512 devices in a mesh: tm: 16 (over z, core), sx: 8 (over y), sy: 4 (over x).
Axes of the slice: x: 4, y: 8, z: 8, core: 2. Of those that a mesh axis runs over, the one named last changes fastest.
Arguments:
- wall_temp: bfloat16 [64, 32768, 128], P('tm', ('sx', 'sy')), may hold values from -6 to 6
- owner_map: int32 [32768, 1], P(('sx', 'sy')), may hold values from 0 to 31; in each aligned block of 1024 rows (0 to 1023, 1024 to 2047, ...) at most 64 rows name the same one
- stencil_column: int32 [32768], P(('sx', 'sy')), may hold values from 0 to 255
- material: int32 [128, 64, 128], P('sx', 'sy'), may hold values from 0 to 3
- conductivity: float32 [4], replicated, may hold values from 0.1 to 1
- capacity: float32 [4], replicated, may hold values from 0.2 to 1
Outputs:
- temperature: float32 [32, 2, 128, 64, 128], P('tm', None, 'sx', 'sy')
The draws below stay inside these ranges and needn't reach their ends.
Inputs may be any that keep to these rules, and one draw needn't show every extreme that they name: `owner_map`: among the 1024 patches of one device (aligned blocks of rows), no owner is named more than 64 times, a bound that some block reaches.
All inputs are finite; a program needn't handle non-finite values.
Results may differ from the reference program's by a relative error of at most 0.0034.
Values may be sent and summed in bfloat16 or wider, within the bound.
No kernel may reach another device: no remote copies, remote signals or barrier semaphores. Data moves between devices by JAX's collectives and lax.ppermute only.
A program may use at most 64 MiB of HBM per device.

```python
import math
import jax
import jax.numpy as jnp
import numpy as np
from jax import lax

TIME = 64
HARM = 32
PW = 128
NMAT = 4
SWEEPS = 4
PATCH_DEV = 1024
BX = 16
BY = 16
OWNERS = 32
CAP = 64
PATCHES = 32768
NX = 128
NY = 64
N_SY = 4


def with_ends(result, stream_key, smallest, top_value):
    place = [jax.random.randint(jax.random.fold_in(stream_key, axis), (), 0, length) for axis, length in enumerate(result.shape)]
    longest = result.shape.index(max(result.shape))
    neighbour = place[:longest] + [(place[longest] + 1) % result.shape[longest]] + place[longest + 1:]
    return result.at[tuple(place)].set(smallest).at[tuple(neighbour)].set(top_value)


def shard_levels(stream_key, shape, cuts, least, top_value):
    def one(dim, parts):
        draws = jax.random.uniform(jax.random.fold_in(jax.random.fold_in(stream_key, 6), dim), (parts,), jnp.float32, least / len(cuts), top_value / len(cuts))
        return jnp.repeat(jnp.exp(draws), shape[dim] // parts).reshape((-1,) + (1,) * (len(shape) - dim - 1))

    gain = one(*cuts[0])
    for cut in cuts[1:]:
        gain = gain * one(*cut)
    return gain


def routed_block(own_key, own, number, rows, count, top, most, skew):
    order = jax.random.permutation(own_key, count)
    crowded, usual = load_shares(count, rows * top, most, skew, True), load_shares(count, rows * top, most, skew, False)
    places = jnp.arange(count)

    def named(tallies, turn):
        used = int((tallies > 0).sum())
        fixed = max(1, used // 4)
        moved = fixed + (places - fixed + turn * (used - fixed)) % max(1, count - fixed)
        return jnp.zeros((count,), jnp.int32).at[order[jnp.where(places < fixed, places, moved)]].set(jnp.asarray(tallies, jnp.int32))

    tallies = jnp.where(number % 4 == 0, named(crowded, number // 4), named(usual, number - number // 4 - 1))
    mixed = jax.random.permutation(jax.random.fold_in(own, 3), count)
    giver, receiver = mixed[0:count // 2 * 2:2], mixed[1:count // 2 * 2:2]
    slack = jnp.minimum(tallies[giver] - 1, most - tallies[receiver]) // 2
    slack = jnp.where((giver == order[0]) | (receiver == order[0]) | (tallies[receiver] == 0), 0, jnp.maximum(slack, 0))
    moved = jax.random.randint(jax.random.fold_in(own, 4), (count // 2,), 0, 1 << 20) % (slack + 1)
    tallies = tallies.at[giver].add(-moved).at[receiver].add(moved)
    items = jnp.searchsorted(jnp.cumsum(tallies), jnp.arange(rows * top), side="right").astype(jnp.int32)
    listing = items.reshape(top, rows).T
    listing = listing[jax.random.permutation(jax.random.fold_in(own, 1), rows)]
    turn = jax.random.randint(jax.random.fold_in(own, 2), (rows, 1), 0, top)
    return jnp.take_along_axis(listing, (jnp.arange(top)[None, :] + turn) % top, axis=1)


def load_shares(number_of, total, reach, slope, full):
    portions = [(1 << 20) // math.isqrt(standing ** slope) + 1 for standing in range(1, number_of + 1)]
    largest = reach if full else min(reach, max(-(-total // number_of), total * portions[0] // sum(portions)))
    least = 1 if total - largest >= number_of - 1 else 0
    holding, surplus = [largest] + [least] * (number_of - 1), total - largest - least * (number_of - 1)
    while surplus > 0:
        movable = [i for i in range(1, number_of) if holding[i] < largest] or [i for i in range(1, number_of) if holding[i] < reach]
        mass, remaining = sum([portions[i] for i in movable]), surplus
        for i in movable:
            extra = min(reach - holding[i], max(1, remaining * portions[i] // mass), surplus)
            holding[i] = holding[i] + extra
            surplus = surplus - extra
    return np.array(holding)


def noise(stream_key, extent, spread, most, shards=(), kind=jnp.bfloat16):
    result = spread * jax.random.normal(stream_key, extent, jnp.float32)
    if shards:
        result = result * shard_levels(stream_key, extent, shards, -0.22, 0.18)
    return jnp.clip(result, -most, most).astype(kind)


def setup_inputs(seed: int = 0) -> dict:
    keys = jax.random.split(jax.random.key(seed), 7)
    wall_temp = noise(keys[0], (TIME, PATCHES, PW), 1.0, 6.0, ((0, 16), (1, 32)))
    owner_map_keys = jax.random.split(jax.random.fold_in(keys[1], 1), PATCHES // PATCH_DEV)
    owner_map_turns = jax.random.permutation(jax.random.fold_in(keys[1], 3), PATCHES // PATCH_DEV)
    owner_map = jax.vmap(lambda own, number: routed_block(jax.random.fold_in(keys[1], 2), own, number, PATCH_DEV, OWNERS, 1, CAP, 2))(owner_map_keys, owner_map_turns).reshape((PATCHES, 1))
    stencil_column = with_ends(jax.random.randint(keys[2], (PATCHES,), 0, BX * BY), jax.random.fold_in(keys[2], 1), 0, (BX * BY) - 1).astype(jnp.int32)
    material = with_ends(jax.random.randint(keys[3], (NX, NY, PW), 0, NMAT), jax.random.fold_in(keys[3], 1), 0, NMAT - 1).astype(jnp.int32)
    conductivity = jnp.clip(jnp.exp(jax.random.uniform(keys[4], (NMAT,), jnp.float32, math.log(0.1), math.log(1.0))), 0.1, 1.0)
    capacity = jnp.clip(jnp.exp(jax.random.uniform(keys[5], (NMAT,), jnp.float32, math.log(0.2), math.log(1.0))), 0.2, 1.0)
    return {"wall_temp": wall_temp, "owner_map": owner_map, "stencil_column": stencil_column, "material": material, "conductivity": conductivity, "capacity": capacity}


omega_step = 0.1

def dft_table():
    freq_index = jnp.arange(HARM, dtype=jnp.int32)
    time_index = jnp.arange(TIME, dtype=jnp.int32)
    phase_int = freq_index[:, None] * time_index[None, :] % TIME
    angles = phase_int.astype(jnp.float32) * jnp.float32(2.0 * math.pi / TIME)
    amplitude = jnp.float32(2.0 / math.sqrt(TIME))
    table_rows = jnp.stack([amplitude * jnp.cos(angles), -amplitude * jnp.sin(angles)], axis=1)
    return table_rows.reshape(2 * HARM, TIME).astype(jnp.bfloat16)

def lookup(material, table):
    values = jnp.zeros(material.shape, jnp.float32)
    for material_id in range(NMAT):
        values = jnp.where(material == material_id, table[material_id], values)
    return values

def face_value(conduct, other):
    other = jnp.where(other > 0, other, conduct)
    return 2.0 * conduct * other / (conduct + other)

def face_values(conduct, padded):
    next_x = face_value(conduct, padded[2:, 1:-1, 1:-1])
    prev_x = face_value(conduct, padded[:-2, 1:-1, 1:-1])
    next_y = face_value(conduct, padded[1:-1, 2:, 1:-1])
    prev_y = face_value(conduct, padded[1:-1, :-2, 1:-1])
    next_z = face_value(conduct, padded[1:-1, 1:-1, 2:])
    prev_z = face_value(conduct, padded[1:-1, 1:-1, :-2])
    total = next_x + prev_x + next_y + prev_y + next_z + prev_z
    return ((next_x, prev_x, next_y, prev_y, next_z, prev_z), total)

def relax_sweep(padded, source, faces, real_den, imag_den):
    next_x, prev_x, next_y, prev_y, next_z, prev_z = faces
    nearby = next_x * padded[..., 2:, 1:-1, 1:-1] + prev_x * padded[..., :-2, 1:-1, 1:-1]
    nearby = nearby + next_y * padded[..., 1:-1, 2:, 1:-1] + prev_y * padded[..., 1:-1, :-2, 1:-1]
    nearby = nearby + next_z * padded[..., 1:-1, 1:-1, 2:] + prev_z * padded[..., 1:-1, 1:-1, :-2]
    numerator = source + nearby
    real_num = numerator[..., 0, :, :, :]
    imag_num = numerator[..., 1, :, :, :]
    modulus = real_den * real_den + imag_den * imag_den
    real_out = (real_num * real_den + imag_num * imag_den) / modulus
    imag_out = (imag_num * real_den - real_num * imag_den) / modulus
    return jnp.stack([real_out, imag_out], axis=-4)

def reference(wall_temp, owner_map, stencil_column, material, conductivity, capacity):
    transform_rows = dft_table()
    flattened = wall_temp.reshape(TIME, PATCHES * PW)
    harmonic = jnp.dot(transform_rows, flattened, preferred_element_type=jnp.float32)
    harmonic = harmonic.astype(jnp.bfloat16).reshape(2 * HARM, PATCHES, PW)
    owner_ids = owner_map[:, 0]
    cell_x = owner_ids // N_SY * BX + stencil_column // BY
    cell_y = owner_ids % N_SY * BY + stencil_column % BY
    target = (cell_x * NY + cell_y).astype(jnp.int32)
    conduct = lookup(material, conductivity)
    heat_cap = lookup(material, capacity)
    rim = jnp.pad(conduct, 1, mode='edge')
    faces, real_den = face_values(conduct, rim)

    def per_harmonic(index):
        pair = lax.dynamic_slice_in_dim(harmonic, 2 * index, 2, 0).astype(jnp.float32)
        summed = jax.ops.segment_sum(jnp.transpose(pair, (1, 0, 2)), target, NX * NY)
        source = jnp.transpose(summed.reshape(NX, NY, 2, PW), (2, 0, 1, 3))
        imag_den = omega_step * index.astype(jnp.float32) * heat_cap
        field = relax_sweep(jnp.zeros((2, NX + 2, NY + 2, PW + 2), jnp.float32), source, faces, real_den, imag_den)
        for sweep in range(SWEEPS - 1):
            padded = jnp.pad(field, ((0, 0), (1, 1), (1, 1), (1, 1)))
            field = relax_sweep(padded, source, faces, real_den, imag_den)
        return field
    return lax.map(per_harmonic, jnp.arange(HARM, dtype=jnp.int32))
```

```python
import math

import jax
import jax.numpy as jnp
import numpy as np
from jax import lax
from jax.experimental import pallas as pl
from jax.experimental.pallas import tpu as pltpu
from jax.sharding import PartitionSpec as P

TIME = 64
HARM = 32
NMAT = 4
CAP = 64
OWNERS = 32
WIDE = 3
Y0 = 8
YE = 32

omega_step = 0.1

F32 = jnp.float32
BF16 = jnp.bfloat16


def dft_table():
    freq_index = jnp.arange(HARM, dtype=jnp.int32)
    time_index = jnp.arange(TIME, dtype=jnp.int32)
    phase_int = freq_index[:, None] * time_index[None, :] % TIME
    angles = phase_int.astype(jnp.float32) * jnp.float32(2.0 * math.pi / TIME)
    amplitude = jnp.float32(2.0 / math.sqrt(TIME))
    table_rows = jnp.stack([amplitude * jnp.cos(angles), -amplitude * jnp.sin(angles)], axis=1)
    return table_rows.reshape(2 * HARM, TIME).astype(jnp.bfloat16)


def iota(shape, dim):
    return lax.broadcasted_iota(jnp.int32, shape, dim)


def pack_kernel(wall_ref, owner_ref, column_ref, out_ref, slot_ref):
    times, count, width = wall_ref.shape
    owner = owner_ref[...]
    hit = owner == iota((OWNERS, count), 0)
    hit_b = hit.astype(F32).astype(BF16)
    before = (iota((count, count), 0) < iota((count, count), 1)).astype(F32).astype(BF16)
    earlier = jnp.dot(hit_b, before, preferred_element_type=F32)
    rank = jnp.sum(jnp.where(hit, earlier, 0.0), axis=0, keepdims=True).astype(jnp.int32)
    slot_ref[...] = owner * CAP + rank
    at_rank = (rank == iota((2 * CAP, count), 0) % CAP).astype(F32).astype(BF16)
    marks = jnp.where(hit, (column_ref[...] + 1).astype(F32), 0.0).astype(BF16)
    columns = lax.dot_general(
        marks, at_rank, (((1,), (1,)), ((), ())), preferred_element_type=F32
    )
    out_ref[:, times * CAP :, :] = jnp.broadcast_to(
        columns[:, None, :], (OWNERS, out_ref.shape[1] - times * CAP, width)
    ).astype(BF16)
    group = 4

    def step(g, _):
        place = (slot_ref[...] - g * (group * CAP) == iota((group * CAP, count), 0)).astype(F32).astype(BF16)
        rows = jnp.concatenate([wall_ref[t] for t in range(times)], axis=1)
        moved = jnp.dot(place, rows, preferred_element_type=F32).astype(BF16)
        for t in range(times):
            out_ref[pl.ds(g * group, group), t * CAP : (t + 1) * CAP, :] = moved[
                :, t * width : (t + 1) * width
            ].reshape(group, CAP, width)
        return 0

    lax.fori_loop(0, OWNERS // group, step, 0)


def sum_kernel(rows_ref, out_ref, *, times, cells):
    width = rows_ref.shape[2]
    side = out_ref.shape[1] // times
    acc = jnp.zeros((cells, times * width), F32)
    low = iota((1, width), 1) < CAP
    for g in range(OWNERS // 4):
        marks, rows = [], []
        for pair in range(2):
            i = g * 4 + pair * 2
            even = rows_ref[i, times * CAP : times * CAP + 8, :].astype(F32)[0:1]
            odd = rows_ref[i + 1, times * CAP : times * CAP + 8, :].astype(F32)[0:1]
            column = jnp.where(low, even, odd).astype(jnp.int32) - 1
            marks.append((column == iota((cells, width), 0)).astype(F32).astype(BF16))
            for j in range(2):
                rows.append(
                    jnp.concatenate(
                        [rows_ref[i + j, t * CAP : (t + 1) * CAP, :] for t in range(times)], axis=1
                    )
                )
        acc = acc + jnp.dot(
            jnp.concatenate(marks, axis=1),
            jnp.concatenate(rows, axis=0),
            preferred_element_type=F32,
        )
    total = acc.astype(BF16)
    for t in range(times):
        out_ref[:, t * side : (t + 1) * side, :] = total[:, t * width : (t + 1) * width].reshape(
            cells // side, side, width
        )


def coef_kernel(omega_ref, conductivity_ref, capacity_ref, ids_ref, fx_ref, fy_ref, fz_ref, a_ref, b_ref, c_ref):
    ext_x, ye, width = ids_ref.shape
    harms = a_ref.shape[1]

    def conduct_step(i, _):
        ids = ids_ref[i]
        value = jnp.zeros((ye, width), F32)
        for m in range(NMAT):
            value = jnp.where(ids == m + 1, conductivity_ref[m], value)
        c_ref[i] = value
        return 0

    lax.fori_loop(0, ext_x, conduct_step, 0)

    def face(a, b):
        return jnp.where(b > 0, 2.0 * a * b / jnp.where(b > 0, a + b, 1.0), a)

    lane = iota((ye, width), 1)

    def fx_step(i, _):
        fx_ref[i] = face(c_ref[i], c_ref[i + 1])
        return 0

    lax.fori_loop(0, ext_x - 1, fx_step, 0)

    def step(i, _):
        c = c_ref[i + 1]
        next_x = fx_ref[i + 1]
        prev_x = face(c, c_ref[i])
        next_y = face(c, pltpu.roll(c, ye - 1, 0))
        prev_y = face(c, pltpu.roll(c, 1, 0))
        next_z = face(c, jnp.where(lane == width - 1, 0.0, pltpu.roll(c, width - 1, 1)))
        prev_z = face(c, jnp.where(lane == 0, 0.0, pltpu.roll(c, 1, 1)))
        real_den = next_x + prev_x + next_y + prev_y + next_z + prev_z
        fy_ref[i] = next_y
        fz_ref[i] = jnp.where(lane == width - 1, 0.0, next_z)
        ids = ids_ref[i + 1]
        heat = jnp.zeros((ye, width), F32)
        for m in range(NMAT):
            heat = jnp.where(ids == m + 1, capacity_ref[m], heat)
        inside = ids > 0
        for h in range(harms):
            imag_den = omega_ref[h] * heat
            modulus = real_den * real_den + imag_den * imag_den
            modulus = jnp.where(inside, modulus, 1.0)
            a_ref[i, h] = jnp.where(inside, real_den / modulus, 0.0)
            b_ref[i, h] = jnp.where(inside, imag_den / modulus, 0.0)
        return 0

    lax.fori_loop(0, ext_x - 2, step, 0)


def solve_kernel(mid_ref, xlo_ref, xhi_ref, ylo_ref, yhi_ref, fx_ref, fy_ref, fz_ref, a_ref, b_ref, out_ref, s_ref, f_ref, g_ref):
    size_x = mid_ref.shape[0]
    wide = xlo_ref.shape[0]
    ext_x, comps, ye, width = s_ref.shape
    harms = comps // 2
    side = mid_ref.shape[1] // comps

    s_ref[...] = jnp.zeros(s_ref.shape, F32)
    for ref, start in ((xlo_ref, 0), (mid_ref, wide), (xhi_ref, wide + size_x)):
        for c in range(comps):
            s_ref[start : start + ref.shape[0], c, Y0 : Y0 + side, :] = ref[
                :, c * side : (c + 1) * side, :
            ].astype(F32)
    for k in range(wide):
        for ref, start in ((ylo_ref, Y0 - wide + k), (yhi_ref, Y0 + side + k)):
            s_ref[:, :, start, :] = ref[k].astype(F32).reshape(ext_x, comps, width)

    def quotient(i, h, real_num, imag_num):
        a = a_ref[i, h]
        b = b_ref[i, h]
        return real_num * a + imag_num * b, imag_num * a - real_num * b

    def first(i, _):
        for h in range(harms):
            real_out, imag_out = quotient(i, h, s_ref[i, 2 * h], s_ref[i, 2 * h + 1])
            f_ref[i, 2 * h] = real_out
            f_ref[i, 2 * h + 1] = imag_out
        return 0

    lax.fori_loop(0, ext_x, first, 0)

    def numerator(src, i, c):
        here = src[i, c]
        fy = fy_ref[i]
        fz = fz_ref[i]
        total = s_ref[i, c] + fx_ref[i + 1] * src[i + 1, c] + fx_ref[i] * src[i - 1, c]
        total = total + fy * pltpu.roll(here, ye - 1, 0) + pltpu.roll(fy * here, 1, 0)
        return total + fz * pltpu.roll(here, width - 1, 1) + pltpu.roll(fz * here, 1, 1)

    def sweep(src, dst, margin):
        def step(i, _):
            for h in range(harms):
                real_out, imag_out = quotient(
                    i, h, numerator(src, i, 2 * h), numerator(src, i, 2 * h + 1)
                )
                dst[i, 2 * h] = real_out
                dst[i, 2 * h + 1] = imag_out
            return 0

        lax.fori_loop(margin, ext_x - margin, step, 0)

    sweep(f_ref, g_ref, 1)
    sweep(g_ref, f_ref, 2)

    def last(i, _):
        for h in range(harms):
            real_out, imag_out = quotient(
                i, h, numerator(f_ref, i, 2 * h), numerator(f_ref, i, 2 * h + 1)
            )
            out_ref[h, 0, i - wide] = real_out[Y0 : Y0 + side]
            out_ref[h, 1, i - wide] = imag_out[Y0 : Y0 + side]
        return 0

    lax.fori_loop(wide, wide + size_x, last, 0)


def swap(block, axis, dim, width):
    count = lax.axis_size(axis)
    forward = [(i, i + 1) for i in range(count - 1)]
    backward = [(target, source) for source, target in forward]
    size = block.shape[dim]
    low = lax.ppermute(lax.slice_in_dim(block, size - width, size, axis=dim), axis, forward)
    high = lax.ppermute(lax.slice_in_dim(block, 0, width, axis=dim), axis, backward)
    return low, high


def body(wall_temp, owner_map, stencil_column, material, conductivity, capacity):
    times, count, width = wall_temp.shape
    size_x, size_y, _ = material.shape
    steps = lax.axis_size("tm")
    comps = 2 * HARM // steps
    harms = comps // 2
    ext_x = size_x + 2 * WIDE
    params = pltpu.CompilerParams(vmem_limit_bytes=48 * 1024 * 1024)
    vmem = pl.BlockSpec(memory_space=pltpu.VMEM)
    smem = pl.BlockSpec(memory_space=pltpu.SMEM)

    packed = pl.pallas_call(
        pack_kernel,
        out_shape=jax.ShapeDtypeStruct((OWNERS, times * CAP + 16, width), BF16),
        in_specs=[vmem] * 3,
        out_specs=vmem,
        scratch_shapes=[pltpu.VMEM((1, count), jnp.int32)],
        compiler_params=params,
        name="pack",
    )(wall_temp, owner_map.reshape(1, count), stencil_column.reshape(1, count))
    received = lax.all_to_all(packed, ("sx", "sy"), split_axis=0, concat_axis=0, tiled=True)

    ids = (material + 1).astype(BF16)
    low, high = swap(ids, "sx", 0, WIDE + 1)
    ids = jnp.concatenate([low, ids, high], axis=0)
    low, high = swap(ids, "sy", 1, WIDE + 1)
    rim = jnp.zeros((ids.shape[0], Y0 - WIDE - 1, width), BF16)
    ids = jnp.concatenate([rim, low, ids, high, rim], axis=1).astype(jnp.int32)
    harm_index = lax.axis_index("tm") * harms + jnp.arange(harms, dtype=jnp.int32)
    omega = omega_step * harm_index.astype(F32)
    fx, fy, fz, quot_a, quot_b = pl.pallas_call(
        coef_kernel,
        out_shape=[
            jax.ShapeDtypeStruct((ext_x + 1, YE, width), F32),
            jax.ShapeDtypeStruct((ext_x, YE, width), F32),
            jax.ShapeDtypeStruct((ext_x, YE, width), F32),
            jax.ShapeDtypeStruct((ext_x, harms, YE, width), F32),
            jax.ShapeDtypeStruct((ext_x, harms, YE, width), F32),
        ],
        in_specs=[smem, smem, smem, vmem],
        out_specs=[vmem] * 5,
        scratch_shapes=[pltpu.VMEM((ext_x + 2, YE, width), F32)],
        compiler_params=params,
        name="coef",
    )(omega, conductivity, capacity, ids)

    cells = size_x * size_y
    sums = pl.pallas_call(
        lambda *refs: sum_kernel(*refs, times=times, cells=cells),
        out_shape=jax.ShapeDtypeStruct((size_x, times * size_y, width), BF16),
        in_specs=[vmem],
        out_specs=vmem,
        compiler_params=params,
        name="cell_sum",
    )(received)
    gathered = lax.all_to_all(sums, "tm", split_axis=0, concat_axis=0, tiled=True)
    weights = jnp.kron(dft_table(), jnp.eye(size_y, dtype=BF16))
    harmonic = jnp.dot(
        weights, gathered.reshape(TIME * size_y, width), preferred_element_type=F32
    ).astype(BF16)
    harmonic = harmonic.reshape(steps, comps * size_y, width)
    source = lax.all_to_all(harmonic, "tm", split_axis=0, concat_axis=0, tiled=True)

    xlo, xhi = swap(source, "sx", 0, WIDE)
    rows = jnp.concatenate([xlo, source, xhi], axis=0).reshape(ext_x, comps, size_y, width)
    rows = jnp.concatenate([rows[:, :, :WIDE], rows[:, :, size_y - WIDE :]], axis=2)
    rows = jnp.transpose(rows, (2, 0, 1, 3)).reshape(2 * WIDE, ext_x * comps, width)
    count_y = lax.axis_size("sy")
    forward = [(i, i + 1) for i in range(count_y - 1)]
    backward = [(target, start) for start, target in forward]
    ylo = lax.ppermute(rows[WIDE:], "sy", forward)
    yhi = lax.ppermute(rows[:WIDE], "sy", backward)
    field = pl.pallas_call(
        solve_kernel,
        out_shape=jax.ShapeDtypeStruct((harms, 2, size_x, size_y, width), F32),
        in_specs=[vmem] * 10,
        out_specs=vmem,
        scratch_shapes=[pltpu.VMEM((ext_x, comps, YE, width), F32)] * 3,
        compiler_params=params,
        name="solve",
    )(source, xlo, xhi, ylo, yhi, fx, fy, fz, quot_a, quot_b)
    return field


def solution(mesh):
    in_specs = (
        P("tm", ("sx", "sy"), None),
        P(("sx", "sy"), None),
        P(("sx", "sy")),
        P("sx", "sy", None),
        P(),
        P(),
    )
    out_specs = P("tm", None, "sx", "sy", None)
    return jax.shard_map(body, mesh=mesh, in_specs=in_specs, out_specs=out_specs, check_vma=False)
```

```python
import math

import jax
import jax.numpy as jnp
from jax import lax
from jax.experimental import pallas as pl
from jax.experimental.pallas import tpu as pltpu
from jax.sharding import PartitionSpec as P

TIME = 64
HARM = 32
NMAT = 4
CAP = 64
OWNERS = 32
WIDE = 3
Y0 = 8
YE = 32

omega_step = 0.1

F32 = jnp.float32
BF16 = jnp.bfloat16


def dft_table():
    freq_index = jnp.arange(HARM, dtype=jnp.int32)
    time_index = jnp.arange(TIME, dtype=jnp.int32)
    phase_int = freq_index[:, None] * time_index[None, :] % TIME
    angles = phase_int.astype(jnp.float32) * jnp.float32(2.0 * math.pi / TIME)
    amplitude = jnp.float32(2.0 / math.sqrt(TIME))
    table_rows = jnp.stack([amplitude * jnp.cos(angles), -amplitude * jnp.sin(angles)], axis=1)
    return table_rows.reshape(2 * HARM, TIME).astype(jnp.bfloat16)


def iota(shape, dim):
    return lax.broadcasted_iota(jnp.int32, shape, dim)


def pack_kernel(wall_ref, owner_ref, column_ref, out_ref, slot_ref):
    times, count, width = wall_ref.shape
    owner = owner_ref[...]
    hit = owner == iota((OWNERS, count), 0)
    hit_b = hit.astype(F32).astype(BF16)
    before = (iota((count, count), 0) < iota((count, count), 1)).astype(F32).astype(BF16)
    earlier = jnp.dot(hit_b, before, preferred_element_type=F32)
    rank = jnp.sum(jnp.where(hit, earlier, 0.0), axis=0, keepdims=True).astype(jnp.int32)
    slot_ref[...] = owner * CAP + rank
    at_rank = (rank == iota((2 * CAP, count), 0) % CAP).astype(F32).astype(BF16)
    marks = jnp.where(hit, (column_ref[...] + 1).astype(F32), 0.0).astype(BF16)
    columns = lax.dot_general(
        marks, at_rank, (((1,), (1,)), ((), ())), preferred_element_type=F32
    )
    out_ref[:, times * CAP :, :] = jnp.broadcast_to(
        columns[:, None, :], (OWNERS, out_ref.shape[1] - times * CAP, width)
    ).astype(BF16)
    group = 4

    def step(g, _):
        place = (slot_ref[...] - g * (group * CAP) == iota((group * CAP, count), 0)).astype(F32).astype(BF16)
        rows = jnp.concatenate([wall_ref[t] for t in range(times)], axis=1)
        moved = jnp.dot(place, rows, preferred_element_type=F32).astype(BF16)
        for t in range(times):
            out_ref[pl.ds(g * group, group), t * CAP : (t + 1) * CAP, :] = moved[
                :, t * width : (t + 1) * width
            ].reshape(group, CAP, width)
        return 0

    lax.fori_loop(0, OWNERS // group, step, 0)


def sum_kernel(rows_ref, out_ref, *, times, cells):
    width = rows_ref.shape[2]
    side = out_ref.shape[1] // times
    acc = jnp.zeros((cells, times * width), F32)
    low = iota((1, width), 1) < CAP
    for g in range(OWNERS // 4):
        marks, rows = [], []
        for pair in range(2):
            i = g * 4 + pair * 2
            even = rows_ref[i, times * CAP : times * CAP + 8, :].astype(F32)[0:1]
            odd = rows_ref[i + 1, times * CAP : times * CAP + 8, :].astype(F32)[0:1]
            column = jnp.where(low, even, odd).astype(jnp.int32) - 1
            marks.append((column == iota((cells, width), 0)).astype(F32).astype(BF16))
            for j in range(2):
                rows.append(
                    jnp.concatenate(
                        [rows_ref[i + j, t * CAP : (t + 1) * CAP, :] for t in range(times)], axis=1
                    )
                )
        acc = acc + jnp.dot(
            jnp.concatenate(marks, axis=1),
            jnp.concatenate(rows, axis=0),
            preferred_element_type=F32,
        )
    total = acc.astype(BF16)
    for t in range(times):
        out_ref[:, t * side : (t + 1) * side, :] = total[:, t * width : (t + 1) * width].reshape(
            cells // side, side, width
        )


def weight_kernel(table_ref, out_ref):
    rows, cols = table_ref.shape
    side = out_ref.shape[0] // rows
    wide = rows * side
    spread = (iota((cols, wide), 1) // side == iota((cols, wide), 0)).astype(F32).astype(BF16)
    lift = (iota((wide, rows), 0) // side == iota((wide, rows), 1)).astype(F32).astype(BF16)
    wider = jnp.dot(table_ref[...], spread, preferred_element_type=F32).astype(BF16)
    step = 256
    for r in range(wide // step):
        full = jnp.dot(lift[r * step : (r + 1) * step], wider, preferred_element_type=F32)
        same = (iota((step, wide), 0) - iota((step, wide), 1)) % side == 0
        out_ref[r * step : (r + 1) * step, :] = jnp.where(same, full, 0.0).astype(BF16)


def dft_kernel(weights_ref, rows_ref, out_ref):
    out_ref[...] = jnp.dot(
        weights_ref[...], rows_ref[...], preferred_element_type=F32
    ).astype(BF16)


def coef_kernel(omega_ref, conductivity_ref, capacity_ref, ids_ref, fx_ref, fy_ref, fz_ref, a_ref, b_ref, c_ref):
    ext_x, ye, width = ids_ref.shape
    harms = a_ref.shape[1]

    def conduct_step(i, _):
        ids = ids_ref[i]
        value = jnp.zeros((ye, width), F32)
        for m in range(NMAT):
            value = jnp.where(ids == m + 1, conductivity_ref[m], value)
        c_ref[i] = value
        return 0

    lax.fori_loop(0, ext_x, conduct_step, 0)

    def face(a, b):
        return jnp.where(b > 0, 2.0 * a * b / jnp.where(b > 0, a + b, 1.0), a)

    lane = iota((ye, width), 1)

    def fx_step(i, _):
        fx_ref[i] = face(c_ref[i], c_ref[i + 1])
        return 0

    lax.fori_loop(0, ext_x - 1, fx_step, 0)

    def step(i, _):
        c = c_ref[i + 1]
        next_x = fx_ref[i + 1]
        prev_x = face(c, c_ref[i])
        next_y = face(c, pltpu.roll(c, ye - 1, 0))
        prev_y = face(c, pltpu.roll(c, 1, 0))
        next_z = face(c, jnp.where(lane == width - 1, 0.0, pltpu.roll(c, width - 1, 1)))
        prev_z = face(c, jnp.where(lane == 0, 0.0, pltpu.roll(c, 1, 1)))
        real_den = next_x + prev_x + next_y + prev_y + next_z + prev_z
        fy_ref[i] = next_y
        fz_ref[i] = jnp.where(lane == width - 1, 0.0, next_z)
        ids = ids_ref[i + 1]
        heat = jnp.zeros((ye, width), F32)
        for m in range(NMAT):
            heat = jnp.where(ids == m + 1, capacity_ref[m], heat)
        inside = ids > 0
        for h in range(harms):
            imag_den = omega_ref[h] * heat
            modulus = real_den * real_den + imag_den * imag_den
            modulus = jnp.where(inside, modulus, 1.0)
            a_ref[i, h] = jnp.where(inside, real_den / modulus, 0.0)
            b_ref[i, h] = jnp.where(inside, imag_den / modulus, 0.0)
        return 0

    lax.fori_loop(0, ext_x - 2, step, 0)


def solve_kernel(mid_ref, xlo_ref, xhi_ref, ylo_ref, yhi_ref, fx_ref, fy_ref, fz_ref, a_ref, b_ref, out_ref, s_ref, f_ref, g_ref):
    size_x = mid_ref.shape[0]
    wide = xlo_ref.shape[0]
    ext_x, comps, ye, width = s_ref.shape
    harms = comps // 2
    side = mid_ref.shape[1] // comps

    s_ref[...] = jnp.zeros(s_ref.shape, F32)
    for ref, start in ((xlo_ref, 0), (mid_ref, wide), (xhi_ref, wide + size_x)):
        for c in range(comps):
            s_ref[start : start + ref.shape[0], c, Y0 : Y0 + side, :] = ref[
                :, c * side : (c + 1) * side, :
            ].astype(F32)
    for k in range(wide):
        for ref, start in ((ylo_ref, Y0 - wide + k), (yhi_ref, Y0 + side + k)):
            s_ref[:, :, start, :] = ref[k].astype(F32).reshape(ext_x, comps, width)

    def quotient(i, h, real_num, imag_num):
        a = a_ref[i, h]
        b = b_ref[i, h]
        return real_num * a + imag_num * b, imag_num * a - real_num * b

    def first(i, _):
        for h in range(harms):
            real_out, imag_out = quotient(i, h, s_ref[i, 2 * h], s_ref[i, 2 * h + 1])
            f_ref[i, 2 * h] = real_out
            f_ref[i, 2 * h + 1] = imag_out
        return 0

    lax.fori_loop(0, ext_x, first, 0)

    def numerator(src, i, c):
        here = src[i, c]
        fy = fy_ref[i]
        fz = fz_ref[i]
        total = s_ref[i, c] + fx_ref[i + 1] * src[i + 1, c] + fx_ref[i] * src[i - 1, c]
        total = total + fy * pltpu.roll(here, ye - 1, 0) + pltpu.roll(fy * here, 1, 0)
        return total + fz * pltpu.roll(here, width - 1, 1) + pltpu.roll(fz * here, 1, 1)

    def sweep(src, dst, margin):
        def step(i, _):
            for h in range(harms):
                real_out, imag_out = quotient(
                    i, h, numerator(src, i, 2 * h), numerator(src, i, 2 * h + 1)
                )
                dst[i, 2 * h] = real_out
                dst[i, 2 * h + 1] = imag_out
            return 0

        lax.fori_loop(margin, ext_x - margin, step, 0)

    sweep(f_ref, g_ref, 1)
    sweep(g_ref, f_ref, 2)

    def last(i, _):
        for h in range(harms):
            real_out, imag_out = quotient(
                i, h, numerator(f_ref, i, 2 * h), numerator(f_ref, i, 2 * h + 1)
            )
            out_ref[h, 0, i - wide] = real_out[Y0 : Y0 + side]
            out_ref[h, 1, i - wide] = imag_out[Y0 : Y0 + side]
        return 0

    lax.fori_loop(wide, wide + size_x, last, 0)


def swap(block, axis, dim, width):
    count = lax.axis_size(axis)
    forward = [(i, i + 1) for i in range(count - 1)]
    backward = [(target, source) for source, target in forward]
    size = block.shape[dim]
    low = lax.ppermute(lax.slice_in_dim(block, size - width, size, axis=dim), axis, forward)
    high = lax.ppermute(lax.slice_in_dim(block, 0, width, axis=dim), axis, backward)
    return low, high


def body(wall_temp, owner_map, stencil_column, material, conductivity, capacity):
    times, count, width = wall_temp.shape
    size_x, size_y, _ = material.shape
    steps = lax.axis_size("tm")
    comps = 2 * HARM // steps
    harms = comps // 2
    ext_x = size_x + 2 * WIDE
    params = pltpu.CompilerParams(vmem_limit_bytes=48 * 1024 * 1024)
    vmem = pl.BlockSpec(memory_space=pltpu.VMEM)
    smem = pl.BlockSpec(memory_space=pltpu.SMEM)

    packed = pl.pallas_call(
        pack_kernel,
        out_shape=jax.ShapeDtypeStruct((OWNERS, times * CAP + 16, width), BF16),
        in_specs=[vmem] * 3,
        out_specs=vmem,
        scratch_shapes=[pltpu.VMEM((1, count), jnp.int32)],
        compiler_params=params,
        name="pack",
    )(wall_temp, owner_map.reshape(1, count), stencil_column.reshape(1, count))
    received = lax.all_to_all(packed, ("sx", "sy"), split_axis=0, concat_axis=0, tiled=True)

    ids = (material + 1).astype(BF16)
    low, high = swap(ids, "sx", 0, WIDE + 1)
    ids = jnp.concatenate([low, ids, high], axis=0)
    low, high = swap(ids, "sy", 1, WIDE + 1)
    rim = jnp.zeros((ids.shape[0], Y0 - WIDE - 1, width), BF16)
    ids = jnp.concatenate([rim, low, ids, high, rim], axis=1).astype(jnp.int32)
    harm_index = lax.axis_index("tm") * harms + jnp.arange(harms, dtype=jnp.int32)
    omega = omega_step * harm_index.astype(F32)
    fx, fy, fz, quot_a, quot_b = pl.pallas_call(
        coef_kernel,
        out_shape=[
            jax.ShapeDtypeStruct((ext_x + 1, YE, width), F32),
            jax.ShapeDtypeStruct((ext_x, YE, width), F32),
            jax.ShapeDtypeStruct((ext_x, YE, width), F32),
            jax.ShapeDtypeStruct((ext_x, harms, YE, width), F32),
            jax.ShapeDtypeStruct((ext_x, harms, YE, width), F32),
        ],
        in_specs=[smem, smem, smem, vmem],
        out_specs=[vmem] * 5,
        scratch_shapes=[pltpu.VMEM((ext_x + 2, YE, width), F32)],
        compiler_params=params,
        name="coef",
    )(omega, conductivity, capacity, ids)

    weights = pl.pallas_call(
        weight_kernel,
        out_shape=jax.ShapeDtypeStruct((TIME * size_y, TIME * size_y), BF16),
        in_specs=[vmem],
        out_specs=vmem,
        compiler_params=params,
        name="weights",
    )(dft_table())
    received, fx, fy, fz, quot_a, quot_b, weights = lax.optimization_barrier(
        (received, fx, fy, fz, quot_a, quot_b, weights)
    )

    cells = size_x * size_y
    sums = pl.pallas_call(
        lambda *refs: sum_kernel(*refs, times=times, cells=cells),
        out_shape=jax.ShapeDtypeStruct((size_x, times * size_y, width), BF16),
        in_specs=[vmem],
        out_specs=vmem,
        compiler_params=params,
        name="cell_sum",
    )(received)
    gathered = lax.all_to_all(sums, "tm", split_axis=0, concat_axis=0, tiled=True)
    harmonic = pl.pallas_call(
        dft_kernel,
        out_shape=jax.ShapeDtypeStruct((TIME * size_y, width), BF16),
        in_specs=[vmem] * 2,
        out_specs=vmem,
        compiler_params=params,
        name="dft",
    )(weights, gathered.reshape(TIME * size_y, width))
    harmonic = harmonic.reshape(steps, comps * size_y, width)
    source = lax.all_to_all(harmonic, "tm", split_axis=0, concat_axis=0, tiled=True)

    xlo, xhi = swap(source, "sx", 0, WIDE)
    rows = jnp.concatenate([xlo, source, xhi], axis=0).reshape(ext_x, comps, size_y, width)
    rows = jnp.concatenate([rows[:, :, :WIDE], rows[:, :, size_y - WIDE :]], axis=2)
    rows = jnp.transpose(rows, (2, 0, 1, 3)).reshape(2 * WIDE, ext_x * comps, width)
    count_y = lax.axis_size("sy")
    forward = [(i, i + 1) for i in range(count_y - 1)]
    backward = [(target, start) for start, target in forward]
    ylo = lax.ppermute(rows[WIDE:], "sy", forward)
    yhi = lax.ppermute(rows[:WIDE], "sy", backward)
    field = pl.pallas_call(
        solve_kernel,
        out_shape=jax.ShapeDtypeStruct((harms, 2, size_x, size_y, width), F32),
        in_specs=[vmem] * 10,
        out_specs=vmem,
        scratch_shapes=[pltpu.VMEM((ext_x, comps, YE, width), F32)] * 3,
        compiler_params=params,
        name="solve",
    )(source, xlo, xhi, ylo, yhi, fx, fy, fz, quot_a, quot_b)
    return field


def solution(mesh):
    in_specs = (
        P("tm", ("sx", "sy"), None),
        P(("sx", "sy"), None),
        P(("sx", "sy")),
        P("sx", "sy", None),
        P(),
        P(),
    )
    out_specs = P("tm", None, "sx", "sy", None)
    return jax.shard_map(body, mesh=mesh, in_specs=in_specs, out_specs=out_specs, check_vma=False)
```

```python
import math

import jax
import jax.numpy as jnp
from jax import lax
from jax.experimental import pallas as pl
from jax.experimental.pallas import tpu as pltpu
from jax.sharding import PartitionSpec as P

TIME = 64
HARM = 32
NMAT = 4
CAP = 64
OWNERS = 32
WIDE = 3
Y0 = 4
YE = 24

omega_step = 0.1

F32 = jnp.float32
BF16 = jnp.bfloat16


def dft_table():
    freq_index = jnp.arange(HARM, dtype=jnp.int32)
    time_index = jnp.arange(TIME, dtype=jnp.int32)
    phase_int = freq_index[:, None] * time_index[None, :] % TIME
    angles = phase_int.astype(jnp.float32) * jnp.float32(2.0 * math.pi / TIME)
    amplitude = jnp.float32(2.0 / math.sqrt(TIME))
    table_rows = jnp.stack([amplitude * jnp.cos(angles), -amplitude * jnp.sin(angles)], axis=1)
    return table_rows.reshape(2 * HARM, TIME).astype(jnp.bfloat16)


def iota(shape, dim):
    return lax.broadcasted_iota(jnp.int32, shape, dim)


def pack_kernel(
    wall_hbm, owner_hbm, column_hbm, out_hbm, wall_ref, owner_ref, column_ref, stage_ref, slot_ref, in_sem, out_sem
):
    times, count, width = wall_ref.shape
    pulls = [
        pltpu.make_async_copy(source, target, in_sem.at[k])
        for k, (source, target) in enumerate(
            ((owner_hbm, owner_ref), (column_hbm, column_ref), (wall_hbm, wall_ref))
        )
    ]
    for pull in pulls:
        pull.start()
    before = (iota((count, count), 0) < iota((count, count), 1)).astype(F32).astype(BF16)
    pulls[0].wait()
    owner = owner_ref[...]
    hit = owner == iota((OWNERS, count), 0)
    hit_b = hit.astype(F32).astype(BF16)
    earlier = jnp.dot(hit_b, before, preferred_element_type=F32)
    rank = jnp.sum(jnp.where(hit, earlier, 0.0), axis=0, keepdims=True).astype(jnp.int32)
    slot_ref[...] = owner * CAP + rank
    pulls[1].wait()
    at_rank = (rank == iota((2 * CAP, count), 0) % CAP).astype(F32).astype(BF16)
    marks = jnp.where(hit, (column_ref[...] + 1).astype(F32), 0.0).astype(BF16)
    columns = lax.dot_general(
        marks, at_rank, (((1,), (1,)), ((), ())), preferred_element_type=F32
    )
    stage_ref[:, times * CAP :, :] = jnp.broadcast_to(
        columns[:, None, :], (OWNERS, stage_ref.shape[1] - times * CAP, width)
    ).astype(BF16)
    pulls[2].wait()
    group = OWNERS // out_sem.shape[0]
    pushes = []
    for g in range(OWNERS // group):
        place = (slot_ref[...] - g * (group * CAP) == iota((group * CAP, count), 0)).astype(F32).astype(BF16)
        rows = jnp.concatenate([wall_ref[t] for t in range(times)], axis=1)
        moved = jnp.dot(place, rows, preferred_element_type=F32).astype(BF16)
        for t in range(times):
            stage_ref[g * group : (g + 1) * group, t * CAP : (t + 1) * CAP, :] = moved[
                :, t * width : (t + 1) * width
            ].reshape(group, CAP, width)
        push = pltpu.make_async_copy(
            stage_ref.at[pl.ds(g * group, group)], out_hbm.at[pl.ds(g * group, group)], out_sem.at[g]
        )
        push.start()
        pushes.append(push)
    for push in pushes:
        push.wait()


def sum_kernel(rows_ref, out_ref, *, times, cells):
    width = rows_ref.shape[2]
    side = out_ref.shape[1] // times
    acc = jnp.zeros((cells, times * width), F32)
    low = iota((1, width), 1) < CAP
    for g in range(OWNERS // 4):
        marks, rows = [], []
        for pair in range(2):
            i = g * 4 + pair * 2
            even = rows_ref[i, times * CAP : times * CAP + 8, :].astype(F32)[0:1]
            odd = rows_ref[i + 1, times * CAP : times * CAP + 8, :].astype(F32)[0:1]
            column = jnp.where(low, even, odd).astype(jnp.int32) - 1
            marks.append((column == iota((cells, width), 0)).astype(F32).astype(BF16))
            for j in range(2):
                rows.append(
                    jnp.concatenate(
                        [rows_ref[i + j, t * CAP : (t + 1) * CAP, :] for t in range(times)], axis=1
                    )
                )
        acc = acc + jnp.dot(
            jnp.concatenate(marks, axis=1),
            jnp.concatenate(rows, axis=0),
            preferred_element_type=F32,
        )
    total = acc.astype(BF16)
    for t in range(times):
        out_ref[:, t * side : (t + 1) * side, :] = total[:, t * width : (t + 1) * width].reshape(
            cells // side, side, width
        )


def weight_kernel(table_ref, out_ref):
    rows, cols = table_ref.shape
    side = out_ref.shape[0] // rows
    wide = rows * side
    spread = (iota((cols, wide), 1) // side == iota((cols, wide), 0)).astype(F32).astype(BF16)
    lift = (iota((wide, rows), 0) // side == iota((wide, rows), 1)).astype(F32).astype(BF16)
    wider = jnp.dot(table_ref[...], spread, preferred_element_type=F32).astype(BF16)
    step = 256
    for r in range(wide // step):
        full = jnp.dot(lift[r * step : (r + 1) * step], wider, preferred_element_type=F32)
        same = (iota((step, wide), 0) - iota((step, wide), 1)) % side == 0
        out_ref[r * step : (r + 1) * step, :] = jnp.where(same, full, 0.0).astype(BF16)


def dft_kernel(weights_ref, rows_ref, out_ref):
    out_ref[...] = jnp.dot(
        weights_ref[...], rows_ref[...], preferred_element_type=F32
    ).astype(BF16)


def coef_kernel(omega_ref, conductivity_ref, capacity_ref, ids_ref, coef_ref, c_ref):
    ext_x, ye, width = ids_ref.shape
    harms = omega_ref.shape[0]

    def table(ids, values):
        value = jnp.zeros((ye, width), F32)
        for m in range(NMAT):
            value = jnp.where(ids == m + 1, values[m], value)
        return value

    def conduct_step(i, _):
        c_ref[i] = table(ids_ref[i], conductivity_ref)
        return 0

    lax.fori_loop(0, ext_x, conduct_step, 0)

    def face(a, b):
        b = jnp.where(b > 0, b, a)
        both = a + b
        return 2.0 * a * b / jnp.where(both > 0, both, 1.0)

    lane = iota((ye, width), 1)

    def step(i, prev_x):
        c = c_ref[i + 1]
        after = c_ref[i + 2]
        next_x = face(c, after)
        next_y = face(c, pltpu.roll(c, ye - 1, 0))
        next_z = face(c, jnp.where(lane == width - 1, 0.0, pltpu.roll(c, width - 1, 1)))
        prev_y = face(c, pltpu.roll(c, 1, 0))
        prev_z = jnp.where(lane == 0, c, pltpu.roll(next_z, 1, 1))
        real_den = next_x + jnp.where(c_ref[i] > 0, prev_x, c) + next_y + prev_y + next_z + prev_z
        coef_ref[i, 0] = next_x
        coef_ref[i, 1] = next_y
        coef_ref[i, 2] = jnp.where(lane == width - 1, 0.0, next_z)
        ids = ids_ref[i + 1]
        heat = table(ids, capacity_ref)
        inside = ids > 0
        for h in range(harms):
            imag_den = omega_ref[h] * heat
            modulus = real_den * real_den + imag_den * imag_den
            inverse = jnp.where(inside, 1.0 / jnp.where(inside, modulus, 1.0), 0.0)
            coef_ref[i, 3 + 2 * h] = real_den * inverse
            coef_ref[i, 4 + 2 * h] = imag_den * inverse
        return next_x

    lax.fori_loop(0, ext_x - 2, step, face(c_ref[0], c_ref[1]))


def solve_kernel(mid_ref, xlo_ref, xhi_ref, ylo_ref, yhi_ref, coef_ref, out_ref, s_ref, f_ref, g_ref):
    size_x = mid_ref.shape[0]
    wide = xlo_ref.shape[0]
    ext_x, comps, ye, width = s_ref.shape
    harms = comps // 2
    side = mid_ref.shape[1] // comps

    edge = jnp.zeros((ext_x, comps, Y0 - wide, width), F32)
    s_ref[:, :, : Y0 - wide, :] = edge
    s_ref[:, :, ye - Y0 + wide :, :] = edge
    for ref, start in ((xlo_ref, 0), (mid_ref, wide), (xhi_ref, wide + size_x)):
        for c in range(comps):
            s_ref[start : start + ref.shape[0], c, Y0 : Y0 + side, :] = ref[
                :, c * side : (c + 1) * side, :
            ].astype(F32)
    for k in range(wide):
        for ref, start in ((ylo_ref, Y0 - wide + k), (yhi_ref, Y0 + side + k)):
            s_ref[:, :, start, :] = ref[k].astype(F32).reshape(ext_x, comps, width)

    def quotient(i, h, real_num, imag_num):
        a = coef_ref[i, 3 + 2 * h]
        b = coef_ref[i, 4 + 2 * h]
        return real_num * a + imag_num * b, imag_num * a - real_num * b

    def pairs(begin, end, row):
        def step(k, _):
            row(begin + 2 * k)
            row(begin + 2 * k + 1)
            return 0

        lax.fori_loop(0, (end - begin) // 2, step, 0)

    def first(i):
        for h in range(harms):
            f_ref[i, 2 * h], f_ref[i, 2 * h + 1] = quotient(i, h, s_ref[i, 2 * h], s_ref[i, 2 * h + 1])

    pairs(0, ext_x, first)

    def numerator(src, i, c):
        here = src[i, c]
        fy = coef_ref[i, 1]
        fz = coef_ref[i, 2]
        total = s_ref[i, c] + coef_ref[i, 0] * src[i + 1, c] + coef_ref[i - 1, 0] * src[i - 1, c]
        total = total + fy * pltpu.roll(here, ye - 1, 0) + pltpu.roll(fy * here, 1, 0)
        return total + fz * pltpu.roll(here, width - 1, 1) + pltpu.roll(fz * here, 1, 1)

    def sweep(src, dst, margin):
        def row(i):
            for h in range(harms):
                dst[i, 2 * h], dst[i, 2 * h + 1] = quotient(
                    i, h, numerator(src, i, 2 * h), numerator(src, i, 2 * h + 1)
                )

        pairs(margin, ext_x - margin, row)

    sweep(f_ref, g_ref, 1)
    sweep(g_ref, f_ref, 2)

    def last(i):
        for h in range(harms):
            real_out, imag_out = quotient(
                i, h, numerator(f_ref, i, 2 * h), numerator(f_ref, i, 2 * h + 1)
            )
            out_ref[h, 0, i - wide] = real_out[Y0 : Y0 + side]
            out_ref[h, 1, i - wide] = imag_out[Y0 : Y0 + side]

    pairs(wide, wide + size_x, last)


def swap(block, axis, dim, width):
    count = lax.axis_size(axis)
    forward = [(i, i + 1) for i in range(count - 1)]
    backward = [(target, source) for source, target in forward]
    size = block.shape[dim]
    low = lax.ppermute(lax.slice_in_dim(block, size - width, size, axis=dim), axis, forward)
    high = lax.ppermute(lax.slice_in_dim(block, 0, width, axis=dim), axis, backward)
    return low, high


def diagonal(dx, dy):
    count_x, count_y = lax.axis_size("sx"), lax.axis_size("sy")
    return [
        (x * count_y + y, (x + dx) * count_y + y + dy)
        for x in range(count_x)
        for y in range(count_y)
        if 0 <= x + dx < count_x and 0 <= y + dy < count_y
    ]


def body(wall_temp, owner_map, stencil_column, material, conductivity, capacity):
    times, count, width = wall_temp.shape
    size_x, size_y, _ = material.shape
    steps = lax.axis_size("tm")
    comps = 2 * HARM // steps
    harms = comps // 2
    ext_x = size_x + 2 * WIDE
    params = pltpu.CompilerParams(vmem_limit_bytes=48 * 1024 * 1024)
    vmem = pl.BlockSpec(memory_space=pltpu.VMEM)
    smem = pl.BlockSpec(memory_space=pltpu.SMEM)

    hbm = pl.BlockSpec(memory_space=pltpu.HBM)
    packed = pl.pallas_call(
        pack_kernel,
        out_shape=pltpu.HBM((OWNERS, times * CAP + 8, width), BF16),
        in_specs=[hbm] * 3,
        out_specs=hbm,
        scratch_shapes=[
            pltpu.VMEM((times, count, width), BF16),
            pltpu.VMEM((1, count), jnp.int32),
            pltpu.VMEM((1, count), jnp.int32),
            pltpu.VMEM((OWNERS, times * CAP + 8, width), BF16),
            pltpu.VMEM((1, count), jnp.int32),
            pltpu.SemaphoreType.DMA((3,)),
            pltpu.SemaphoreType.DMA((8,)),
        ],
        compiler_params=params,
        name="pack",
    )(
        *(
            pltpu.with_memory_space_constraint(operand, pltpu.HBM)
            for operand in (wall_temp, owner_map.reshape(1, count), stencil_column.reshape(1, count))
        )
    )
    received = lax.all_to_all(packed, ("sx", "sy"), split_axis=0, concat_axis=0, tiled=True)

    ids = (material + 1).astype(BF16)
    west, east = swap(ids, "sx", 0, Y0)
    south, north = swap(ids, "sy", 1, Y0)
    corner = {}
    for dx in (1, -1):
        for dy in (1, -1):
            part = ids[size_x - Y0 :] if dx > 0 else ids[:Y0]
            part = part[:, size_y - Y0 :] if dy > 0 else part[:, :Y0]
            corner[dx, dy] = lax.ppermute(part, ("sx", "sy"), diagonal(dx, dy))
    received, west, east, south, north, corner = lax.optimization_barrier(
        (received, west, east, south, north, corner)
    )
    ids = jnp.concatenate(
        [
            jnp.concatenate([corner[1, 1], west, corner[1, -1]], axis=1),
            jnp.concatenate([south, ids, north], axis=1),
            jnp.concatenate([corner[-1, 1], east, corner[-1, -1]], axis=1),
        ],
        axis=0,
    ).astype(jnp.int32)
    harm_index = lax.axis_index("tm") * harms + jnp.arange(harms, dtype=jnp.int32)
    omega = omega_step * harm_index.astype(F32)
    coef = pl.pallas_call(
        coef_kernel,
        out_shape=jax.ShapeDtypeStruct((ext_x, 3 + 2 * harms, YE, width), F32),
        in_specs=[smem, smem, smem, vmem],
        out_specs=vmem,
        scratch_shapes=[pltpu.VMEM((ext_x + 2, YE, width), F32)],
        compiler_params=params,
        name="coef",
    )(omega, conductivity, capacity, ids)

    weights = pl.pallas_call(
        weight_kernel,
        out_shape=jax.ShapeDtypeStruct((TIME * size_y, TIME * size_y), BF16),
        in_specs=[vmem],
        out_specs=vmem,
        compiler_params=params,
        name="weights",
    )(dft_table())
    received, weights = lax.optimization_barrier((received, weights))

    cells = size_x * size_y
    sums = pl.pallas_call(
        lambda *refs: sum_kernel(*refs, times=times, cells=cells),
        out_shape=jax.ShapeDtypeStruct((size_x, times * size_y, width), BF16),
        in_specs=[vmem],
        out_specs=vmem,
        compiler_params=params,
        name="cell_sum",
    )(received)
    gathered = lax.all_to_all(sums, "tm", split_axis=0, concat_axis=0, tiled=True)
    gathered, coef = lax.optimization_barrier((gathered, coef))
    harmonic = pl.pallas_call(
        dft_kernel,
        out_shape=jax.ShapeDtypeStruct((TIME * size_y, width), BF16),
        in_specs=[vmem] * 2,
        out_specs=vmem,
        compiler_params=params,
        name="dft",
    )(weights, gathered.reshape(TIME * size_y, width))
    harmonic = harmonic.reshape(steps, comps * size_y, width)
    source = lax.all_to_all(harmonic, "tm", split_axis=0, concat_axis=0, tiled=True)

    xlo, xhi = swap(source, "sx", 0, WIDE)
    rows = jnp.concatenate([xlo, source, xhi], axis=0).reshape(ext_x, comps, size_y, width)
    rows = jnp.concatenate([rows[:, :, :WIDE], rows[:, :, size_y - WIDE :]], axis=2)
    rows = jnp.transpose(rows, (2, 0, 1, 3)).reshape(2 * WIDE, ext_x * comps, width)
    count_y = lax.axis_size("sy")
    forward = [(i, i + 1) for i in range(count_y - 1)]
    backward = [(target, start) for start, target in forward]
    ylo = lax.ppermute(rows[WIDE:], "sy", forward)
    yhi = lax.ppermute(rows[:WIDE], "sy", backward)
    field = pl.pallas_call(
        solve_kernel,
        out_shape=jax.ShapeDtypeStruct((harms, 2, size_x, size_y, width), F32),
        in_specs=[vmem] * 6,
        out_specs=vmem,
        scratch_shapes=[pltpu.VMEM((ext_x, comps, YE, width), F32)] * 3,
        compiler_params=params,
        name="solve",
    )(source, xlo, xhi, ylo, yhi, coef)
    return field


def solution(mesh):
    in_specs = (
        P("tm", ("sx", "sy"), None),
        P(("sx", "sy"), None),
        P(("sx", "sy")),
        P("sx", "sy", None),
        P(),
        P(),
    )
    out_specs = P("tm", None, "sx", "sy", None)
    return jax.shard_map(body, mesh=mesh, in_specs=in_specs, out_specs=out_specs, check_vma=False)
```

```python
import math

import jax
import jax.numpy as jnp
from jax import lax
from jax.experimental import pallas as pl
from jax.experimental.pallas import tpu as pltpu
from jax.sharding import PartitionSpec as P

TIME = 64
HARM = 32
NMAT = 4
CAP = 64
OWNERS = 32
WIDE = 3
Y0 = 4
YE = 24

omega_step = 0.1

F32 = jnp.float32
BF16 = jnp.bfloat16


def dft_table():
    freq_index = jnp.arange(HARM, dtype=jnp.int32)
    time_index = jnp.arange(TIME, dtype=jnp.int32)
    phase_int = freq_index[:, None] * time_index[None, :] % TIME
    angles = phase_int.astype(jnp.float32) * jnp.float32(2.0 * math.pi / TIME)
    amplitude = jnp.float32(2.0 / math.sqrt(TIME))
    table_rows = jnp.stack([amplitude * jnp.cos(angles), -amplitude * jnp.sin(angles)], axis=1)
    return table_rows.reshape(2 * HARM, TIME).astype(jnp.bfloat16)


def iota(shape, dim):
    return lax.broadcasted_iota(jnp.int32, shape, dim)


def pack_kernel(
    wall_hbm, owner_hbm, column_hbm, out_hbm, wall_ref, owner_ref, column_ref, stage_ref, slot_ref, in_sem, out_sem
):
    times, count, width = wall_ref.shape
    pulls = [
        pltpu.make_async_copy(source, target, in_sem.at[k])
        for k, (source, target) in enumerate(
            ((owner_hbm, owner_ref), (column_hbm, column_ref), (wall_hbm, wall_ref))
        )
    ]
    for pull in pulls:
        pull.start()
    before = (iota((count, count), 0) < iota((count, count), 1)).astype(F32).astype(BF16)
    pulls[0].wait()
    owner = owner_ref[...]
    hit = owner == iota((OWNERS, count), 0)
    hit_b = hit.astype(F32).astype(BF16)
    earlier = jnp.dot(hit_b, before, preferred_element_type=F32)
    rank = jnp.sum(jnp.where(hit, earlier, 0.0), axis=0, keepdims=True).astype(jnp.int32)
    slot_ref[...] = owner * CAP + rank
    pulls[1].wait()
    at_rank = (rank == iota((2 * CAP, count), 0) % CAP).astype(F32).astype(BF16)
    marks = jnp.where(hit, (column_ref[...] + 1).astype(F32), 0.0).astype(BF16)
    columns = lax.dot_general(
        marks, at_rank, (((1,), (1,)), ((), ())), preferred_element_type=F32
    )
    stage_ref[:, times * CAP :, :] = jnp.broadcast_to(
        columns[:, None, :], (OWNERS, stage_ref.shape[1] - times * CAP, width)
    ).astype(BF16)
    pulls[2].wait()
    group = OWNERS // out_sem.shape[0]
    pushes = []
    for g in range(OWNERS // group):
        place = (slot_ref[...] - g * (group * CAP) == iota((group * CAP, count), 0)).astype(F32).astype(BF16)
        rows = jnp.concatenate([wall_ref[t] for t in range(times)], axis=1)
        moved = jnp.dot(place, rows, preferred_element_type=F32).astype(BF16)
        for t in range(times):
            stage_ref[g * group : (g + 1) * group, t * CAP : (t + 1) * CAP, :] = moved[
                :, t * width : (t + 1) * width
            ].reshape(group, CAP, width)
        push = pltpu.make_async_copy(
            stage_ref.at[pl.ds(g * group, group)], out_hbm.at[pl.ds(g * group, group)], out_sem.at[g]
        )
        push.start()
        pushes.append(push)
    for push in pushes:
        push.wait()


def sum_kernel(rows_ref, out_ref, *, times, cells):
    width = rows_ref.shape[2]
    side = out_ref.shape[1] // times
    acc = jnp.zeros((cells, times * width), F32)
    low = iota((1, width), 1) < CAP
    for g in range(OWNERS // 4):
        marks, rows = [], []
        for pair in range(2):
            i = g * 4 + pair * 2
            even = rows_ref[i, times * CAP : times * CAP + 8, :].astype(F32)[0:1]
            odd = rows_ref[i + 1, times * CAP : times * CAP + 8, :].astype(F32)[0:1]
            column = jnp.where(low, even, odd).astype(jnp.int32) - 1
            marks.append((column == iota((cells, width), 0)).astype(F32).astype(BF16))
            for j in range(2):
                rows.append(
                    jnp.concatenate(
                        [rows_ref[i + j, t * CAP : (t + 1) * CAP, :] for t in range(times)], axis=1
                    )
                )
        acc = acc + jnp.dot(
            jnp.concatenate(marks, axis=1),
            jnp.concatenate(rows, axis=0),
            preferred_element_type=F32,
        )
    total = acc.astype(BF16)
    for t in range(times):
        out_ref[:, t * side : (t + 1) * side, :] = total[:, t * width : (t + 1) * width].reshape(
            cells // side, side, width
        )


def weight_kernel(table_ref, out_ref):
    rows, cols = table_ref.shape
    side = out_ref.shape[0] // rows
    wide = rows * side
    spread = (iota((cols, wide), 1) // side == iota((cols, wide), 0)).astype(F32).astype(BF16)
    lift = (iota((wide, rows), 0) // side == iota((wide, rows), 1)).astype(F32).astype(BF16)
    wider = jnp.dot(table_ref[...], spread, preferred_element_type=F32).astype(BF16)
    step = 256
    for r in range(wide // step):
        full = jnp.dot(lift[r * step : (r + 1) * step], wider, preferred_element_type=F32)
        same = (iota((step, wide), 0) - iota((step, wide), 1)) % side == 0
        out_ref[r * step : (r + 1) * step, :] = jnp.where(same, full, 0.0).astype(BF16)


def dft_kernel(weights_ref, rows_ref, out_ref):
    out_ref[...] = jnp.dot(
        weights_ref[...], rows_ref[...], preferred_element_type=F32
    ).astype(BF16)


def coef_kernel(omega_ref, conductivity_ref, capacity_ref, ids_ref, coef_ref, c_ref):
    ext_x, ye, width = ids_ref.shape
    harms = omega_ref.shape[0]

    def table(ids, values):
        value = jnp.zeros((ye, width), F32)
        for m in range(NMAT):
            value = jnp.where(ids == m + 1, values[m], value)
        return value

    def conduct_step(i, _):
        c_ref[i] = table(ids_ref[i], conductivity_ref)
        return 0

    lax.fori_loop(0, ext_x, conduct_step, 0)

    def face(a, b):
        b = jnp.where(b > 0, b, a)
        both = a + b
        return 2.0 * a * b / jnp.where(both > 0, both, 1.0)

    lane = iota((ye, width), 1)

    def step(i, prev_x):
        c = c_ref[i + 1]
        after = c_ref[i + 2]
        next_x = face(c, after)
        next_y = face(c, pltpu.roll(c, ye - 1, 0))
        next_z = face(c, jnp.where(lane == width - 1, 0.0, pltpu.roll(c, width - 1, 1)))
        prev_y = face(c, pltpu.roll(c, 1, 0))
        prev_z = jnp.where(lane == 0, c, pltpu.roll(next_z, 1, 1))
        real_den = next_x + jnp.where(c_ref[i] > 0, prev_x, c) + next_y + prev_y + next_z + prev_z
        coef_ref[i, 0] = next_x
        coef_ref[i, 1] = next_y
        coef_ref[i, 2] = jnp.where(lane == width - 1, 0.0, next_z)
        ids = ids_ref[i + 1]
        heat = table(ids, capacity_ref)
        inside = ids > 0
        for h in range(harms):
            imag_den = omega_ref[h] * heat
            modulus = real_den * real_den + imag_den * imag_den
            inverse = jnp.where(inside, 1.0 / jnp.where(inside, modulus, 1.0), 0.0)
            coef_ref[i, 3 + 2 * h] = real_den * inverse
            coef_ref[i, 4 + 2 * h] = imag_den * inverse
        return next_x

    lax.fori_loop(0, ext_x - 2, step, face(c_ref[0], c_ref[1]))


def solve_kernel(mid_ref, xlo_ref, xhi_ref, ylo_ref, yhi_ref, coef_ref, out_ref, s_ref, f_ref, g_ref):
    size_x = mid_ref.shape[0]
    wide = xlo_ref.shape[0]
    ext_x, comps, ye, width = s_ref.shape
    harms = comps // 2
    side = mid_ref.shape[1] // comps

    edge = jnp.zeros((ext_x, comps, Y0 - wide, width), F32)
    s_ref[:, :, : Y0 - wide, :] = edge
    s_ref[:, :, ye - Y0 + wide :, :] = edge
    for ref, start in ((xlo_ref, 0), (mid_ref, wide), (xhi_ref, wide + size_x)):
        for c in range(comps):
            s_ref[start : start + ref.shape[0], c, Y0 : Y0 + side, :] = ref[
                :, c * side : (c + 1) * side, :
            ].astype(F32)
    for k in range(wide):
        for ref, start in ((ylo_ref, Y0 - wide + k), (yhi_ref, Y0 + side + k)):
            s_ref[:, :, start, :] = ref[k].astype(F32).reshape(ext_x, comps, width)

    def quotient(i, h, real_num, imag_num):
        a = coef_ref[i, 3 + 2 * h]
        b = coef_ref[i, 4 + 2 * h]
        return real_num * a + imag_num * b, imag_num * a - real_num * b

    def pairs(begin, end, row):
        def step(k, _):
            row(begin + 2 * k)
            row(begin + 2 * k + 1)
            return 0

        lax.fori_loop(0, (end - begin) // 2, step, 0)

    def first(i):
        for h in range(harms):
            f_ref[i, 2 * h], f_ref[i, 2 * h + 1] = quotient(i, h, s_ref[i, 2 * h], s_ref[i, 2 * h + 1])

    pairs(0, ext_x, first)

    def numerator(src, i, c):
        here = src[i, c]
        fy = coef_ref[i, 1]
        fz = coef_ref[i, 2]
        total = s_ref[i, c] + coef_ref[i, 0] * src[i + 1, c] + coef_ref[i - 1, 0] * src[i - 1, c]
        total = total + fy * pltpu.roll(here, ye - 1, 0) + pltpu.roll(fy * here, 1, 0)
        return total + fz * pltpu.roll(here, width - 1, 1) + pltpu.roll(fz * here, 1, 1)

    def sweep(src, dst, margin):
        def row(i):
            for h in range(harms):
                dst[i, 2 * h], dst[i, 2 * h + 1] = quotient(
                    i, h, numerator(src, i, 2 * h), numerator(src, i, 2 * h + 1)
                )

        pairs(margin, ext_x - margin, row)

    sweep(f_ref, g_ref, 1)
    sweep(g_ref, f_ref, 2)

    def last(i):
        for h in range(harms):
            real_out, imag_out = quotient(
                i, h, numerator(f_ref, i, 2 * h), numerator(f_ref, i, 2 * h + 1)
            )
            out_ref[h, 0, i - wide] = real_out[Y0 : Y0 + side]
            out_ref[h, 1, i - wide] = imag_out[Y0 : Y0 + side]

    pairs(wide, wide + size_x, last)


def swap(block, axis, dim, width):
    count = lax.axis_size(axis)
    forward = [(i, i + 1) for i in range(count - 1)]
    backward = [(target, source) for source, target in forward]
    size = block.shape[dim]
    low = lax.ppermute(lax.slice_in_dim(block, size - width, size, axis=dim), axis, forward)
    high = lax.ppermute(lax.slice_in_dim(block, 0, width, axis=dim), axis, backward)
    return low, high


def body(wall_temp, owner_map, stencil_column, material, conductivity, capacity):
    times, count, width = wall_temp.shape
    size_x, size_y, _ = material.shape
    steps = lax.axis_size("tm")
    comps = 2 * HARM // steps
    harms = comps // 2
    ext_x = size_x + 2 * WIDE
    params = pltpu.CompilerParams(vmem_limit_bytes=48 * 1024 * 1024)
    vmem = pl.BlockSpec(memory_space=pltpu.VMEM)
    smem = pl.BlockSpec(memory_space=pltpu.SMEM)

    hbm = pl.BlockSpec(memory_space=pltpu.HBM)
    packed = pl.pallas_call(
        pack_kernel,
        out_shape=pltpu.HBM((OWNERS, times * CAP + 8, width), BF16),
        in_specs=[hbm] * 3,
        out_specs=hbm,
        scratch_shapes=[
            pltpu.VMEM((times, count, width), BF16),
            pltpu.VMEM((1, count), jnp.int32),
            pltpu.VMEM((1, count), jnp.int32),
            pltpu.VMEM((OWNERS, times * CAP + 8, width), BF16),
            pltpu.VMEM((1, count), jnp.int32),
            pltpu.SemaphoreType.DMA((3,)),
            pltpu.SemaphoreType.DMA((8,)),
        ],
        compiler_params=params,
        name="pack",
    )(
        *(
            pltpu.with_memory_space_constraint(operand, pltpu.HBM)
            for operand in (wall_temp, owner_map.reshape(1, count), stencil_column.reshape(1, count))
        )
    )
    received = lax.all_to_all(packed, ("sx", "sy"), split_axis=0, concat_axis=0, tiled=True)

    table, material = lax.optimization_barrier((dft_table(), material))
    weights = pl.pallas_call(
        weight_kernel,
        out_shape=jax.ShapeDtypeStruct((TIME * size_y, TIME * size_y), BF16),
        in_specs=[vmem],
        out_specs=vmem,
        compiler_params=params,
        name="weights",
    )(table)
    material, weights = lax.optimization_barrier((material, weights))
    ids = (material + 1).astype(BF16)
    west, east = swap(ids, "sx", 0, Y0)
    received, west, east = lax.optimization_barrier((received, west, east))
    ids = jnp.concatenate([west, ids, east], axis=0)
    south, north = swap(ids, "sy", 1, Y0)
    cells = size_x * size_y
    sums = pl.pallas_call(
        lambda *refs: sum_kernel(*refs, times=times, cells=cells),
        out_shape=jax.ShapeDtypeStruct((size_x, times * size_y, width), BF16),
        in_specs=[vmem],
        out_specs=vmem,
        compiler_params=params,
        name="cell_sum",
    )(received)
    gathered = lax.all_to_all(sums, "tm", split_axis=0, concat_axis=0, tiled=True)
    gathered, ids, south, north = lax.optimization_barrier((gathered, ids, south, north))
    ids = jnp.concatenate([south, ids, north], axis=1).astype(jnp.int32)
    harm_index = lax.axis_index("tm") * harms + jnp.arange(harms, dtype=jnp.int32)
    omega = omega_step * harm_index.astype(F32)
    coef = pl.pallas_call(
        coef_kernel,
        out_shape=jax.ShapeDtypeStruct((ext_x, 3 + 2 * harms, YE, width), F32),
        in_specs=[smem, smem, smem, vmem],
        out_specs=vmem,
        scratch_shapes=[pltpu.VMEM((ext_x + 2, YE, width), F32)],
        compiler_params=params,
        name="coef",
    )(omega, conductivity, capacity, ids)
    harmonic = pl.pallas_call(
        dft_kernel,
        out_shape=jax.ShapeDtypeStruct((TIME * size_y, width), BF16),
        in_specs=[vmem] * 2,
        out_specs=vmem,
        compiler_params=params,
        name="dft",
    )(weights, gathered.reshape(TIME * size_y, width))
    harmonic = harmonic.reshape(steps, comps * size_y, width)
    source = lax.all_to_all(harmonic, "tm", split_axis=0, concat_axis=0, tiled=True)
    source, coef = lax.optimization_barrier((source, coef))

    xlo, xhi = swap(source, "sx", 0, WIDE)
    rows = jnp.concatenate([xlo, source, xhi], axis=0).reshape(ext_x, comps, size_y, width)
    rows = jnp.concatenate([rows[:, :, :WIDE], rows[:, :, size_y - WIDE :]], axis=2)
    rows = jnp.transpose(rows, (2, 0, 1, 3)).reshape(2 * WIDE, ext_x * comps, width)
    count_y = lax.axis_size("sy")
    forward = [(i, i + 1) for i in range(count_y - 1)]
    backward = [(target, start) for start, target in forward]
    ylo = lax.ppermute(rows[WIDE:], "sy", forward)
    yhi = lax.ppermute(rows[:WIDE], "sy", backward)
    field = pl.pallas_call(
        solve_kernel,
        out_shape=jax.ShapeDtypeStruct((harms, 2, size_x, size_y, width), F32),
        in_specs=[vmem] * 6,
        out_specs=vmem,
        scratch_shapes=[pltpu.VMEM((ext_x, comps, YE, width), F32)] * 3,
        compiler_params=params,
        name="solve",
    )(source, xlo, xhi, ylo, yhi, coef)
    return field


def solution(mesh):
    in_specs = (
        P("tm", ("sx", "sy"), None),
        P(("sx", "sy"), None),
        P(("sx", "sy")),
        P("sx", "sy", None),
        P(),
        P(),
    )
    out_specs = P("tm", None, "sx", "sy", None)
    return jax.shard_map(body, mesh=mesh, in_specs=in_specs, out_specs=out_specs, check_vma=False)
```

```python
import math

import jax
import jax.numpy as jnp
from jax import lax
from jax.experimental import pallas as pl
from jax.experimental.pallas import tpu as pltpu
from jax.sharding import PartitionSpec as P

TIME = 64
HARM = 32
NMAT = 4
CAP = 64
OWNERS = 32
WIDE = 3
Y0 = 4
YE = 24

omega_step = 0.1

F32 = jnp.float32
BF16 = jnp.bfloat16


def dft_table():
    freq_index = jnp.arange(HARM, dtype=jnp.int32)
    time_index = jnp.arange(TIME, dtype=jnp.int32)
    phase_int = freq_index[:, None] * time_index[None, :] % TIME
    angles = phase_int.astype(jnp.float32) * jnp.float32(2.0 * math.pi / TIME)
    amplitude = jnp.float32(2.0 / math.sqrt(TIME))
    table_rows = jnp.stack([amplitude * jnp.cos(angles), -amplitude * jnp.sin(angles)], axis=1)
    return table_rows.reshape(2 * HARM, TIME).astype(jnp.bfloat16)


def iota(shape, dim):
    return lax.broadcasted_iota(jnp.int32, shape, dim)


def pack_kernel(
    wall_hbm, owner_hbm, column_hbm, out_hbm, wall_ref, owner_ref, column_ref, stage_ref, in_sem, out_sem
):
    times, count, width = wall_ref.shape
    pulls = [
        pltpu.make_async_copy(source, target, in_sem.at[k])
        for k, (source, target) in enumerate(
            ((owner_hbm, owner_ref), (column_hbm, column_ref), (wall_hbm, wall_ref))
        )
    ]
    for pull in pulls:
        pull.start()
    before = (iota((count, count), 0) < iota((count, count), 1)).astype(F32).astype(BF16)
    pulls[0].wait()
    owner = owner_ref[...]
    hit = owner == iota((OWNERS, count), 0)
    hit_b = hit.astype(F32).astype(BF16)
    earlier = jnp.dot(hit_b, before, preferred_element_type=F32)
    rank = jnp.sum(jnp.where(hit, earlier, 0.0), axis=0, keepdims=True).astype(jnp.int32)
    pulls[1].wait()
    half = (rank == iota((CAP, count), 0)).astype(F32).astype(BF16)
    at_rank = jnp.concatenate([half, half], axis=0)
    marks = jnp.where(hit, (column_ref[...] + 1).astype(F32), 0.0).astype(BF16)
    columns = lax.dot_general(
        marks, at_rank, (((1,), (1,)), ((), ())), preferred_element_type=F32
    )
    stage_ref[:, times * CAP :, :] = jnp.broadcast_to(
        columns[:, None, :], (OWNERS, stage_ref.shape[1] - times * CAP, width)
    ).astype(BF16)
    pulls[2].wait()
    group = OWNERS // out_sem.shape[0]
    pushes = []
    for g in range(OWNERS // group):
        place = jnp.concatenate(
            [half * hit_b[o : o + 1, :] for o in range(g * group, (g + 1) * group)], axis=0
        )
        rows = jnp.concatenate([wall_ref[t] for t in range(times)], axis=1)
        moved = jnp.dot(place, rows, preferred_element_type=F32).astype(BF16)
        for t in range(times):
            stage_ref[g * group : (g + 1) * group, t * CAP : (t + 1) * CAP, :] = moved[
                :, t * width : (t + 1) * width
            ].reshape(group, CAP, width)
        push = pltpu.make_async_copy(
            stage_ref.at[pl.ds(g * group, group)], out_hbm.at[pl.ds(g * group, group)], out_sem.at[g]
        )
        push.start()
        pushes.append(push)
    for push in pushes:
        push.wait()


def sum_kernel(rows_ref, out_ref, *, times, cells):
    width = rows_ref.shape[2]
    side = out_ref.shape[1] // times
    acc = jnp.zeros((cells, times * width), F32)
    low = iota((1, width), 1) < CAP
    for g in range(OWNERS // 4):
        marks, rows = [], []
        for pair in range(2):
            i = g * 4 + pair * 2
            even = rows_ref[i, times * CAP : times * CAP + 8, :].astype(F32)[0:1]
            odd = rows_ref[i + 1, times * CAP : times * CAP + 8, :].astype(F32)[0:1]
            column = jnp.where(low, even, odd).astype(jnp.int32) - 1
            marks.append((column == iota((cells, width), 0)).astype(F32).astype(BF16))
            for j in range(2):
                rows.append(
                    jnp.concatenate(
                        [rows_ref[i + j, t * CAP : (t + 1) * CAP, :] for t in range(times)], axis=1
                    )
                )
        acc = acc + jnp.dot(
            jnp.concatenate(marks, axis=1),
            jnp.concatenate(rows, axis=0),
            preferred_element_type=F32,
        )
    total = acc.astype(BF16)
    for t in range(times):
        out_ref[:, t * side : (t + 1) * side, :] = total[:, t * width : (t + 1) * width].reshape(
            cells // side, side, width
        )


def weight_kernel(table_ref, out_ref):
    rows, cols = table_ref.shape
    side = out_ref.shape[0] // rows
    wide = rows * side
    spread = (iota((cols, wide), 1) // side == iota((cols, wide), 0)).astype(F32).astype(BF16)
    lift = (iota((wide, rows), 0) // side == iota((wide, rows), 1)).astype(F32).astype(BF16)
    wider = jnp.dot(table_ref[...], spread, preferred_element_type=F32).astype(BF16)
    step = 256
    for r in range(wide // step):
        full = jnp.dot(lift[r * step : (r + 1) * step], wider, preferred_element_type=F32)
        same = (iota((step, wide), 0) - iota((step, wide), 1)) % side == 0
        out_ref[r * step : (r + 1) * step, :] = jnp.where(same, full, 0.0).astype(BF16)


def dft_kernel(weights_ref, rows_ref, out_ref):
    times, side, width = rows_ref.shape
    half = side // 2
    rows = rows_ref[...].astype(F32)
    rows = jnp.concatenate(
        [rows[:, :half].reshape(times * half, width), rows[:, half:].reshape(times * half, width)], axis=1
    ).astype(BF16)
    made = jnp.dot(weights_ref[...], rows, preferred_element_type=F32)
    made = jnp.concatenate(
        [made[:, :width].reshape(times, half, width), made[:, width:].reshape(times, half, width)], axis=1
    )
    out_ref[...] = made.astype(BF16)


def coef_kernel(omega_ref, conductivity_ref, capacity_ref, ids_ref, coef_ref, c_ref):
    ext_x, ye, width = ids_ref.shape
    harms = omega_ref.shape[0]

    def table(ids, values):
        value = jnp.zeros((ye, width), F32)
        for m in range(NMAT):
            value = jnp.where(ids == m + 1, values[m], value)
        return value

    def conduct_step(i, _):
        c_ref[i] = table(ids_ref[i], conductivity_ref)
        return 0

    lax.fori_loop(0, ext_x, conduct_step, 0)

    def face(a, b):
        b = jnp.where(b > 0, b, a)
        both = a + b
        return 2.0 * a * b / jnp.where(both > 0, both, 1.0)

    lane = iota((ye, width), 1)

    def step(i, prev_x):
        c = c_ref[i + 1]
        after = c_ref[i + 2]
        next_x = face(c, after)
        next_y = face(c, pltpu.roll(c, ye - 1, 0))
        next_z = face(c, jnp.where(lane == width - 1, 0.0, pltpu.roll(c, width - 1, 1)))
        prev_y = face(c, pltpu.roll(c, 1, 0))
        prev_z = jnp.where(lane == 0, c, pltpu.roll(next_z, 1, 1))
        real_den = next_x + jnp.where(c_ref[i] > 0, prev_x, c) + next_y + prev_y + next_z + prev_z
        coef_ref[i, 0] = next_x
        coef_ref[i, 1] = next_y
        coef_ref[i, 2] = jnp.where(lane == width - 1, 0.0, next_z)
        ids = ids_ref[i + 1]
        heat = table(ids, capacity_ref)
        inside = ids > 0
        for h in range(harms):
            imag_den = omega_ref[h] * heat
            modulus = real_den * real_den + imag_den * imag_den
            inverse = jnp.where(inside, 1.0 / jnp.where(inside, modulus, 1.0), 0.0)
            coef_ref[i, 3 + 2 * h] = real_den * inverse
            coef_ref[i, 4 + 2 * h] = imag_den * inverse
        return next_x

    lax.fori_loop(0, ext_x - 2, step, face(c_ref[0], c_ref[1]))


def solve_kernel(mid_ref, xlo_ref, xhi_ref, ylo_ref, yhi_ref, coef_ref, out_ref, s_ref, f_ref, g_ref):
    size_x = mid_ref.shape[0]
    wide = xlo_ref.shape[0]
    ext_x, comps, ye, width = s_ref.shape
    harms = comps // 2
    side = mid_ref.shape[1] // comps

    edge = jnp.zeros((ext_x, comps, Y0 - wide, width), F32)
    s_ref[:, :, : Y0 - wide, :] = edge
    s_ref[:, :, ye - Y0 + wide :, :] = edge
    for ref, start in ((xlo_ref, 0), (mid_ref, wide), (xhi_ref, wide + size_x)):
        for c in range(comps):
            s_ref[start : start + ref.shape[0], c, Y0 : Y0 + side, :] = ref[
                :, c * side : (c + 1) * side, :
            ].astype(F32)
    for k in range(wide):
        for ref, start in ((ylo_ref, Y0 - wide + k), (yhi_ref, Y0 + side + k)):
            s_ref[:, :, start, :] = ref[k].astype(F32).reshape(ext_x, comps, width)

    def quotient(i, h, real_num, imag_num):
        a = coef_ref[i, 3 + 2 * h]
        b = coef_ref[i, 4 + 2 * h]
        return real_num * a + imag_num * b, imag_num * a - real_num * b

    def pairs(begin, end, row):
        def step(k, _):
            row(begin + 2 * k)
            row(begin + 2 * k + 1)
            return 0

        lax.fori_loop(0, (end - begin) // 2, step, 0)

    def first(i):
        for h in range(harms):
            f_ref[i, 2 * h], f_ref[i, 2 * h + 1] = quotient(i, h, s_ref[i, 2 * h], s_ref[i, 2 * h + 1])

    pairs(0, ext_x, first)

    def numerator(src, i, c):
        here = src[i, c]
        fy = coef_ref[i, 1]
        fz = coef_ref[i, 2]
        total = s_ref[i, c] + coef_ref[i, 0] * src[i + 1, c] + coef_ref[i - 1, 0] * src[i - 1, c]
        total = total + fy * pltpu.roll(here, ye - 1, 0) + pltpu.roll(fy * here, 1, 0)
        return total + fz * pltpu.roll(here, width - 1, 1) + pltpu.roll(fz * here, 1, 1)

    def sweep(src, dst, margin):
        def row(i):
            for h in range(harms):
                dst[i, 2 * h], dst[i, 2 * h + 1] = quotient(
                    i, h, numerator(src, i, 2 * h), numerator(src, i, 2 * h + 1)
                )

        pairs(margin, ext_x - margin, row)

    sweep(f_ref, g_ref, 1)
    sweep(g_ref, f_ref, 2)

    def last(i):
        for h in range(harms):
            real_out, imag_out = quotient(
                i, h, numerator(f_ref, i, 2 * h), numerator(f_ref, i, 2 * h + 1)
            )
            out_ref[h, 0, i - wide] = real_out[Y0 : Y0 + side]
            out_ref[h, 1, i - wide] = imag_out[Y0 : Y0 + side]

    pairs(wide, wide + size_x, last)


def swap(block, axis, dim, width):
    count = lax.axis_size(axis)
    forward = [(i, i + 1) for i in range(count - 1)]
    backward = [(target, source) for source, target in forward]
    size = block.shape[dim]
    low = lax.ppermute(lax.slice_in_dim(block, size - width, size, axis=dim), axis, forward)
    high = lax.ppermute(lax.slice_in_dim(block, 0, width, axis=dim), axis, backward)
    return low, high


def body(wall_temp, owner_map, stencil_column, material, conductivity, capacity):
    times, count, width = wall_temp.shape
    size_x, size_y, _ = material.shape
    steps = lax.axis_size("tm")
    comps = 2 * HARM // steps
    harms = comps // 2
    ext_x = size_x + 2 * WIDE
    params = pltpu.CompilerParams(vmem_limit_bytes=16 * 1024 * 1024)
    vmem = pl.BlockSpec(memory_space=pltpu.VMEM)
    smem = pl.BlockSpec(memory_space=pltpu.SMEM)

    hbm = pl.BlockSpec(memory_space=pltpu.HBM)
    packed = pl.pallas_call(
        pack_kernel,
        out_shape=pltpu.HBM((OWNERS, times * CAP + 8, width), BF16),
        in_specs=[hbm] * 3,
        out_specs=hbm,
        scratch_shapes=[
            pltpu.VMEM((times, count, width), BF16),
            pltpu.VMEM((1, count), jnp.int32),
            pltpu.VMEM((1, count), jnp.int32),
            pltpu.VMEM((OWNERS, times * CAP + 8, width), BF16),
            pltpu.SemaphoreType.DMA((3,)),
            pltpu.SemaphoreType.DMA((8,)),
        ],
        compiler_params=params,
        name="pack",
    )(
        *(
            pltpu.with_memory_space_constraint(operand, pltpu.HBM)
            for operand in (wall_temp, owner_map.reshape(1, count), stencil_column.reshape(1, count))
        )
    )
    received = lax.all_to_all(packed, ("sx", "sy"), split_axis=0, concat_axis=0, tiled=True)

    table, material = lax.optimization_barrier((dft_table(), material))
    weights = pl.pallas_call(
        weight_kernel,
        out_shape=jax.ShapeDtypeStruct((TIME * size_y // 2, TIME * size_y // 2), BF16),
        in_specs=[vmem],
        out_specs=vmem,
        compiler_params=params,
        name="weights",
    )(table)
    material, weights = lax.optimization_barrier((material, weights))
    ids = (material + 1).astype(BF16)
    west, east = swap(ids, "sx", 0, Y0)
    received, west, east = lax.optimization_barrier((received, west, east))
    ids = jnp.concatenate([west, ids, east], axis=0)
    south, north = swap(ids, "sy", 1, Y0)
    cells = size_x * size_y
    sums = pl.pallas_call(
        lambda *refs: sum_kernel(*refs, times=times, cells=cells),
        out_shape=jax.ShapeDtypeStruct((size_x, times * size_y, width), BF16),
        in_specs=[vmem],
        out_specs=vmem,
        compiler_params=params,
        name="cell_sum",
    )(received)
    gathered = lax.all_to_all(sums, "tm", split_axis=0, concat_axis=0, tiled=True)
    gathered, ids, south, north = lax.optimization_barrier((gathered, ids, south, north))
    ids = jnp.concatenate([south, ids, north], axis=1).astype(jnp.int32)
    harm_index = lax.axis_index("tm") * harms + jnp.arange(harms, dtype=jnp.int32)
    omega = omega_step * harm_index.astype(F32)
    coef = pl.pallas_call(
        coef_kernel,
        out_shape=jax.ShapeDtypeStruct((ext_x, 3 + 2 * harms, YE, width), F32),
        in_specs=[smem, smem, smem, vmem],
        out_specs=vmem,
        scratch_shapes=[pltpu.VMEM((ext_x + 2, YE, width), F32)],
        compiler_params=params,
        name="coef",
    )(omega, conductivity, capacity, ids)
    harmonic = pl.pallas_call(
        dft_kernel,
        out_shape=jax.ShapeDtypeStruct((TIME, size_y, width), BF16),
        in_specs=[vmem] * 2,
        out_specs=vmem,
        compiler_params=params,
        name="dft",
    )(weights, gathered.reshape(TIME, size_y, width))
    harmonic = harmonic.reshape(steps, comps * size_y, width)
    source = lax.all_to_all(harmonic, "tm", split_axis=0, concat_axis=0, tiled=True)
    source, coef = lax.optimization_barrier((source, coef))

    xlo, xhi = swap(source, "sx", 0, WIDE)
    rows = jnp.concatenate([xlo, source, xhi], axis=0).reshape(ext_x, comps, size_y, width)
    rows = jnp.concatenate([rows[:, :, :WIDE], rows[:, :, size_y - WIDE :]], axis=2)
    rows = jnp.transpose(rows, (2, 0, 1, 3)).reshape(2 * WIDE, ext_x * comps, width)
    count_y = lax.axis_size("sy")
    forward = [(i, i + 1) for i in range(count_y - 1)]
    backward = [(target, start) for start, target in forward]
    ylo = lax.ppermute(rows[WIDE:], "sy", forward)
    yhi = lax.ppermute(rows[:WIDE], "sy", backward)
    field = pl.pallas_call(
        solve_kernel,
        out_shape=jax.ShapeDtypeStruct((harms, 2, size_x, size_y, width), F32),
        in_specs=[vmem] * 6,
        out_specs=vmem,
        scratch_shapes=[pltpu.VMEM((ext_x, comps, YE, width), F32)] * 3,
        compiler_params=params,
        name="solve",
    )(source, xlo, xhi, ylo, yhi, coef)
    return field


def solution(mesh):
    in_specs = (
        P("tm", ("sx", "sy"), None),
        P(("sx", "sy"), None),
        P(("sx", "sy")),
        P("sx", "sy", None),
        P(),
        P(),
    )
    out_specs = P("tm", None, "sx", "sy", None)
    return jax.shard_map(body, mesh=mesh, in_specs=in_specs, out_specs=out_specs, check_vma=False)
```

```python
import math

import jax
import jax.numpy as jnp
from jax import lax
from jax.experimental import pallas as pl
from jax.experimental.pallas import tpu as pltpu
from jax.sharding import PartitionSpec as P

TIME = 64
HARM = 32
NMAT = 4
CAP = 64
OWNERS = 32
WIDE = 3
Y0 = 4
YE = 24

omega_step = 0.1

F32 = jnp.float32
BF16 = jnp.bfloat16


def dft_table():
    freq_index = jnp.arange(HARM, dtype=jnp.int32)
    time_index = jnp.arange(TIME, dtype=jnp.int32)
    phase_int = freq_index[:, None] * time_index[None, :] % TIME
    angles = phase_int.astype(jnp.float32) * jnp.float32(2.0 * math.pi / TIME)
    amplitude = jnp.float32(2.0 / math.sqrt(TIME))
    table_rows = jnp.stack([amplitude * jnp.cos(angles), -amplitude * jnp.sin(angles)], axis=1)
    return table_rows.reshape(2 * HARM, TIME).astype(jnp.bfloat16)


def iota(shape, dim):
    return lax.broadcasted_iota(jnp.int32, shape, dim)


def pack_kernel(
    wall_hbm, owner_hbm, column_hbm, out_hbm, wall_ref, owner_ref, column_ref, stage_ref, in_sem, out_sem
):
    times, count, width = wall_ref.shape
    pulls = [
        pltpu.make_async_copy(source, target, in_sem.at[k])
        for k, (source, target) in enumerate(
            ((owner_hbm, owner_ref), (column_hbm, column_ref), (wall_hbm, wall_ref))
        )
    ]
    for pull in pulls:
        pull.start()
    before = (iota((width, width), 0) < iota((width, width), 1)).astype(F32).astype(BF16)
    pulls[0].wait()
    owner = owner_ref[...]
    hit = owner == iota((OWNERS, count), 0)
    hit_b = hit.astype(F32).astype(BF16)
    blocks = [hit_b[:, k * width : (k + 1) * width] for k in range(count // width)]
    earlier = jnp.dot(jnp.concatenate(blocks, axis=0), before, preferred_element_type=F32)
    carry = jnp.zeros((OWNERS, 1), F32)
    ranks = []
    for k, block in enumerate(blocks):
        inside = block.astype(F32)
        prefix = earlier[k * OWNERS : (k + 1) * OWNERS] + carry
        ranks.append(jnp.sum(inside * prefix, axis=0, keepdims=True))
        carry = carry + jnp.sum(inside, axis=1, keepdims=True)
    rank = jnp.concatenate(ranks, axis=1).astype(jnp.int32)
    pulls[1].wait()
    half = (rank == iota((CAP, count), 0)).astype(F32).astype(BF16)
    at_rank = jnp.concatenate([half, half], axis=0)
    marks = jnp.where(hit, (column_ref[...] + 1).astype(F32), 0.0).astype(BF16)
    columns = lax.dot_general(
        marks, at_rank, (((1,), (1,)), ((), ())), preferred_element_type=F32
    )
    stage_ref[:, times * CAP :, :] = jnp.broadcast_to(
        columns[:, None, :], (OWNERS, stage_ref.shape[1] - times * CAP, width)
    ).astype(BF16)
    pulls[2].wait()
    group = OWNERS // out_sem.shape[0]
    pushes = []
    for g in range(OWNERS // group):
        place = jnp.concatenate(
            [half * hit_b[o : o + 1, :] for o in range(g * group, (g + 1) * group)], axis=0
        )
        rows = jnp.concatenate([wall_ref[t] for t in range(times)], axis=1)
        moved = jnp.dot(place, rows, preferred_element_type=F32).astype(BF16)
        for t in range(times):
            stage_ref[g * group : (g + 1) * group, t * CAP : (t + 1) * CAP, :] = moved[
                :, t * width : (t + 1) * width
            ].reshape(group, CAP, width)
        push = pltpu.make_async_copy(
            stage_ref.at[pl.ds(g * group, group)], out_hbm.at[pl.ds(g * group, group)], out_sem.at[g]
        )
        push.start()
        pushes.append(push)
    for push in pushes:
        push.wait()


def sum_kernel(rows_ref, out_ref, *, times, cells):
    width = rows_ref.shape[2]
    side = out_ref.shape[1] // times
    acc = jnp.zeros((cells, times * width), F32)
    low = iota((1, width), 1) < CAP
    for g in range(OWNERS // 4):
        marks, rows = [], []
        for pair in range(2):
            i = g * 4 + pair * 2
            even = rows_ref[i, times * CAP : times * CAP + 8, :].astype(F32)[0:1]
            odd = rows_ref[i + 1, times * CAP : times * CAP + 8, :].astype(F32)[0:1]
            column = jnp.where(low, even, odd).astype(jnp.int32) - 1
            marks.append((column == iota((cells, width), 0)).astype(F32).astype(BF16))
            for j in range(2):
                rows.append(
                    jnp.concatenate(
                        [rows_ref[i + j, t * CAP : (t + 1) * CAP, :] for t in range(times)], axis=1
                    )
                )
        acc = acc + jnp.dot(
            jnp.concatenate(marks, axis=1),
            jnp.concatenate(rows, axis=0),
            preferred_element_type=F32,
        )
    total = acc.astype(BF16)
    for t in range(times):
        out_ref[:, t * side : (t + 1) * side, :] = total[:, t * width : (t + 1) * width].reshape(
            cells // side, side, width
        )


def weight_kernel(table_ref, out_ref):
    rows, cols = table_ref.shape
    side = out_ref.shape[0] // rows
    wide = rows * side
    spread = (iota((cols, wide), 1) // side == iota((cols, wide), 0)).astype(F32).astype(BF16)
    lift = (iota((wide, rows), 0) // side == iota((wide, rows), 1)).astype(F32).astype(BF16)
    wider = jnp.dot(table_ref[...], spread, preferred_element_type=F32).astype(BF16)
    step = 256
    for r in range(wide // step):
        full = jnp.dot(lift[r * step : (r + 1) * step], wider, preferred_element_type=F32)
        same = (iota((step, wide), 0) - iota((step, wide), 1)) % side == 0
        out_ref[r * step : (r + 1) * step, :] = jnp.where(same, full, 0.0).astype(BF16)


def dft_kernel(weights_ref, rows_ref, out_ref):
    times, side, width = rows_ref.shape
    half = side // 2
    rows = rows_ref[...].astype(F32)
    rows = jnp.concatenate(
        [rows[:, :half].reshape(times * half, width), rows[:, half:].reshape(times * half, width)], axis=1
    ).astype(BF16)
    made = jnp.dot(weights_ref[...], rows, preferred_element_type=F32)
    made = jnp.concatenate(
        [made[:, :width].reshape(times, half, width), made[:, width:].reshape(times, half, width)], axis=1
    )
    out_ref[...] = made.astype(BF16)


def coef_kernel(omega_ref, conductivity_ref, capacity_ref, ids_ref, coef_ref, c_ref):
    ext_x, ye, width = ids_ref.shape
    harms = omega_ref.shape[0]

    def table(ids, values):
        value = jnp.zeros((ye, width), F32)
        for m in range(NMAT):
            value = jnp.where(ids == m + 1, values[m], value)
        return value

    def conduct_step(i, _):
        c_ref[i] = table(ids_ref[i], conductivity_ref)
        return 0

    lax.fori_loop(0, ext_x, conduct_step, 0)

    def face(a, b):
        b = jnp.where(b > 0, b, a)
        both = a + b
        return 2.0 * a * b / jnp.where(both > 0, both, 1.0)

    lane = iota((ye, width), 1)

    def step(i, prev_x):
        c = c_ref[i + 1]
        after = c_ref[i + 2]
        next_x = face(c, after)
        next_y = face(c, pltpu.roll(c, ye - 1, 0))
        next_z = face(c, jnp.where(lane == width - 1, 0.0, pltpu.roll(c, width - 1, 1)))
        prev_y = face(c, pltpu.roll(c, 1, 0))
        prev_z = jnp.where(lane == 0, c, pltpu.roll(next_z, 1, 1))
        real_den = next_x + jnp.where(c_ref[i] > 0, prev_x, c) + next_y + prev_y + next_z + prev_z
        coef_ref[i, 0] = next_x
        coef_ref[i, 1] = next_y
        coef_ref[i, 2] = jnp.where(lane == width - 1, 0.0, next_z)
        ids = ids_ref[i + 1]
        heat = table(ids, capacity_ref)
        inside = ids > 0
        for h in range(harms):
            imag_den = omega_ref[h] * heat
            modulus = real_den * real_den + imag_den * imag_den
            inverse = jnp.where(inside, 1.0 / jnp.where(inside, modulus, 1.0), 0.0)
            coef_ref[i, 3 + 2 * h] = real_den * inverse
            coef_ref[i, 4 + 2 * h] = imag_den * inverse
        return next_x

    lax.fori_loop(0, ext_x - 2, step, face(c_ref[0], c_ref[1]))


def widen_kernel(mid_ref, ylo_ref, yhi_ref, s_ref, first_ref, last_ref):
    size_x, comps, ye, width = s_ref.shape
    wide = ylo_ref.shape[0]
    side = mid_ref.shape[1] // comps
    edge = jnp.zeros((size_x, comps, Y0 - wide, width), F32)
    s_ref[:, :, : Y0 - wide, :] = edge
    s_ref[:, :, ye - Y0 + wide :, :] = edge
    for c in range(comps):
        s_ref[:, c, Y0 : Y0 + side, :] = mid_ref[:, c * side : (c + 1) * side, :].astype(F32)
    for k in range(wide):
        for ref, start in ((ylo_ref, Y0 - wide + k), (yhi_ref, Y0 + side + k)):
            s_ref[:, :, start, :] = ref[k].astype(F32).reshape(size_x, comps, width)
    first_ref[...] = s_ref[:wide].reshape(wide, comps * ye, width).astype(BF16)
    last_ref[...] = s_ref[size_x - wide :].reshape(wide, comps * ye, width).astype(BF16)


def quotient(coef_ref, i, h, real_num, imag_num):
    a = coef_ref[i, 3 + 2 * h]
    b = coef_ref[i, 4 + 2 * h]
    return real_num * a + imag_num * b, imag_num * a - real_num * b


def sweep_row(coef_ref, source, field, i):
    ye, width = coef_ref.shape[2:]

    def numerator(c):
        here = field(i, c)
        fy = coef_ref[i, 1]
        fz = coef_ref[i, 2]
        total = source(c) + coef_ref[i, 0] * field(i + 1, c) + coef_ref[i - 1, 0] * field(i - 1, c)
        total = total + fy * pltpu.roll(here, ye - 1, 0) + pltpu.roll(fy * here, 1, 0)
        return total + fz * pltpu.roll(here, width - 1, 1) + pltpu.roll(fz * here, 1, 1)

    made = []
    for h in range((coef_ref.shape[1] - 3) // 2):
        made.extend(quotient(coef_ref, i, h, numerator(2 * h), numerator(2 * h + 1)))
    return made


def inner_kernel(s_ref, coef_ref, f1_ref, f2_ref, f3_ref, out_ref, *, wide):
    size_x, comps, ye, width = s_ref.shape
    side = out_ref.shape[3]

    def pairs(begin, end, row):
        def step(k, _):
            row(begin + 2 * k)
            row(begin + 2 * k + 1)
            return 0

        lax.fori_loop(0, (end - begin) // 2, step, 0)

    def first(x):
        for h in range(comps // 2):
            f1_ref[x, 2 * h], f1_ref[x, 2 * h + 1] = quotient(
                coef_ref, x + wide, h, s_ref[x, 2 * h], s_ref[x, 2 * h + 1]
            )

    pairs(0, size_x, first)

    def made(src, x):
        return sweep_row(
            coef_ref, lambda c: s_ref[x, c], lambda i, c: src[i - wide, c], x + wide
        )

    def sweep(src, dst, margin):
        def row(x):
            for c, value in enumerate(made(src, x)):
                dst[x, c] = value

        pairs(margin, size_x - margin, row)

    sweep(f1_ref, f2_ref, 1)
    sweep(f2_ref, f3_ref, 2)

    def last(x):
        for c, value in enumerate(made(f3_ref, x)):
            out_ref[c // 2, c % 2, x - wide] = value[Y0 : Y0 + side]

    pairs(wide, size_x - wide, last)


def outer_kernel(
    xlo_ref, xhi_ref, s_ref, f1_ref, f2_ref, f3_ref, inner_ref, coef_ref, out_hbm, s_rim, g1_ref, g2_ref, g3_ref, rim_ref, sem
):
    size_x, comps, ye, width = s_ref.shape
    wide = xlo_ref.shape[0]
    side = rim_ref.shape[4]
    ext_x = size_x + 2 * wide
    inner = pltpu.make_async_copy(
        inner_ref, out_hbm.at[:, :, pl.ds(wide, size_x - 2 * wide)], sem.at[0]
    )
    inner.start()
    span = 2 * wide + 1

    base = (0, ext_x - span)
    s_rim[0, :wide] = xlo_ref[...].astype(F32).reshape(wide, comps, ye, width)
    s_rim[0, wide : 2 * wide] = s_ref[:wide]
    s_rim[1, wide + 1 :] = xhi_ref[...].astype(F32).reshape(wide, comps, ye, width)
    s_rim[1, 1 : wide + 1] = s_ref[size_x - wide :]
    g1_ref[0, wide : wide + 2] = f1_ref[:2]
    g1_ref[1, wide - 1 : wide + 1] = f1_ref[size_x - 2 :]
    g2_ref[0, wide + 1 : wide + 3] = f2_ref[1:3]
    g2_ref[1, wide - 2 : wide] = f2_ref[size_x - 3 : size_x - 1]
    g3_ref[0, wide + 2 : wide + 4] = f3_ref[2:4]
    g3_ref[1, wide - 3 : wide - 1] = f3_ref[size_x - 4 : size_x - 2]

    def first(k, _):
        for part, j in ((0, k), (1, wide + 1 + k)):
            for h in range(comps // 2):
                g1_ref[part, j, 2 * h], g1_ref[part, j, 2 * h + 1] = quotient(
                    coef_ref, base[part] + j, h, s_rim[part, j, 2 * h], s_rim[part, j, 2 * h + 1]
                )
        return 0

    lax.fori_loop(0, wide, first, 0)

    def made(src, part, j):
        return sweep_row(
            coef_ref,
            lambda c: s_rim[part, j, c],
            lambda i, c: src[part, i - base[part], c],
            base[part] + j,
        )

    def sweep(src, dst, margin):
        def step(k, _):
            for part, j in ((0, margin + k), (1, wide + 1 - margin + k)):
                for c, value in enumerate(made(src, part, j)):
                    dst[part, j, c] = value
            return 0

        lax.fori_loop(0, wide, step, 0)

    sweep(g1_ref, g2_ref, 1)
    sweep(g2_ref, g3_ref, 2)

    def last(k, _):
        for part, j in ((0, wide + k), (1, 1 + k)):
            for c, value in enumerate(made(g3_ref, part, j)):
                rim_ref[part, c // 2, c % 2, k] = value[Y0 : Y0 + side]
        return 0

    lax.fori_loop(0, wide, last, 0)
    low = pltpu.make_async_copy(rim_ref.at[0], out_hbm.at[:, :, pl.ds(0, wide)], sem.at[1])
    high = pltpu.make_async_copy(rim_ref.at[1], out_hbm.at[:, :, pl.ds(size_x - wide, wide)], sem.at[2])
    low.start()
    high.start()
    inner.wait()
    low.wait()
    high.wait()


def swap(block, axis, dim, width):
    count = lax.axis_size(axis)
    forward = [(i, i + 1) for i in range(count - 1)]
    backward = [(target, source) for source, target in forward]
    size = block.shape[dim]
    low = lax.ppermute(lax.slice_in_dim(block, size - width, size, axis=dim), axis, forward)
    high = lax.ppermute(lax.slice_in_dim(block, 0, width, axis=dim), axis, backward)
    return low, high


def body(wall_temp, owner_map, stencil_column, material, conductivity, capacity):
    times, count, width = wall_temp.shape
    size_x, size_y, _ = material.shape
    steps = lax.axis_size("tm")
    comps = 2 * HARM // steps
    harms = comps // 2
    ext_x = size_x + 2 * WIDE
    params = pltpu.CompilerParams(vmem_limit_bytes=16 * 1024 * 1024)
    vmem = pl.BlockSpec(memory_space=pltpu.VMEM)
    smem = pl.BlockSpec(memory_space=pltpu.SMEM)

    hbm = pl.BlockSpec(memory_space=pltpu.HBM)
    packed = pl.pallas_call(
        pack_kernel,
        out_shape=pltpu.HBM((OWNERS, times * CAP + 8, width), BF16),
        in_specs=[hbm] * 3,
        out_specs=hbm,
        scratch_shapes=[
            pltpu.VMEM((times, count, width), BF16),
            pltpu.VMEM((1, count), jnp.int32),
            pltpu.VMEM((1, count), jnp.int32),
            pltpu.VMEM((OWNERS, times * CAP + 8, width), BF16),
            pltpu.SemaphoreType.DMA((3,)),
            pltpu.SemaphoreType.DMA((8,)),
        ],
        compiler_params=params,
        name="pack",
    )(
        *(
            pltpu.with_memory_space_constraint(operand, pltpu.HBM)
            for operand in (wall_temp, owner_map.reshape(1, count), stencil_column.reshape(1, count))
        )
    )
    received = lax.all_to_all(packed, ("sx", "sy"), split_axis=0, concat_axis=0, tiled=True)

    table, material = lax.optimization_barrier((dft_table(), material))
    weights = pl.pallas_call(
        weight_kernel,
        out_shape=jax.ShapeDtypeStruct((TIME * size_y // 2, TIME * size_y // 2), BF16),
        in_specs=[vmem],
        out_specs=vmem,
        compiler_params=params,
        name="weights",
    )(table)
    material, weights = lax.optimization_barrier((material, weights))
    ids = (material + 1).astype(BF16)
    west, east = swap(ids, "sx", 0, Y0)
    received, west, east = lax.optimization_barrier((received, west, east))
    ids = jnp.concatenate([west, ids, east], axis=0)
    south, north = swap(ids, "sy", 1, Y0)
    cells = size_x * size_y
    sums = pl.pallas_call(
        lambda *refs: sum_kernel(*refs, times=times, cells=cells),
        out_shape=jax.ShapeDtypeStruct((size_x, times * size_y, width), BF16),
        in_specs=[vmem],
        out_specs=vmem,
        compiler_params=params,
        name="cell_sum",
    )(received)
    gathered = lax.all_to_all(sums, "tm", split_axis=0, concat_axis=0, tiled=True)
    gathered, ids, south, north = lax.optimization_barrier((gathered, ids, south, north))
    ids = jnp.concatenate([south, ids, north], axis=1).astype(jnp.int32)
    harmonic = pl.pallas_call(
        dft_kernel,
        out_shape=jax.ShapeDtypeStruct((TIME, size_y, width), BF16),
        in_specs=[vmem] * 2,
        out_specs=vmem,
        compiler_params=params,
        name="dft",
    )(weights, gathered.reshape(TIME, size_y, width))
    harmonic = harmonic.reshape(steps, comps * size_y, width)
    source = lax.all_to_all(harmonic, "tm", split_axis=0, concat_axis=0, tiled=True)
    source, ids = lax.optimization_barrier((source, ids))

    rows = source.reshape(size_x, comps, size_y, width)
    rows = jnp.concatenate([rows[:, :, :WIDE], rows[:, :, size_y - WIDE :]], axis=2)
    rows = jnp.transpose(rows, (2, 0, 1, 3)).reshape(2 * WIDE, size_x * comps, width)
    ylo, yhi = swap(rows, "sy", 0, WIDE)
    harm_index = lax.axis_index("tm") * harms + jnp.arange(harms, dtype=jnp.int32)
    omega = omega_step * harm_index.astype(F32)
    coef = pl.pallas_call(
        coef_kernel,
        out_shape=jax.ShapeDtypeStruct((ext_x, 3 + 2 * harms, YE, width), F32),
        in_specs=[smem, smem, smem, vmem],
        out_specs=vmem,
        scratch_shapes=[pltpu.VMEM((ext_x + 2, YE, width), F32)],
        compiler_params=params,
        name="coef",
    )(omega, conductivity, capacity, ids)
    ylo, yhi, coef = lax.optimization_barrier((ylo, yhi, coef))
    widened = jax.ShapeDtypeStruct((size_x, comps, YE, width), F32)
    strip = jax.ShapeDtypeStruct((WIDE, comps * YE, width), BF16)
    source, first_rows, last_rows = pl.pallas_call(
        widen_kernel,
        out_shape=[widened, strip, strip],
        in_specs=[vmem] * 3,
        out_specs=[vmem] * 3,
        compiler_params=params,
        name="widen",
    )(source, ylo, yhi)
    count_x = lax.axis_size("sx")
    forward = [(i, i + 1) for i in range(count_x - 1)]
    backward = [(target, start) for start, target in forward]
    xlo = lax.ppermute(last_rows, "sx", forward)
    xhi = lax.ppermute(first_rows, "sx", backward)
    field1, field2, field3, inner = pl.pallas_call(
        lambda *refs: inner_kernel(*refs, wide=WIDE),
        out_shape=[widened] * 3
        + [jax.ShapeDtypeStruct((harms, 2, size_x - 2 * WIDE, size_y, width), F32)],
        in_specs=[vmem] * 2,
        out_specs=[vmem] * 4,
        compiler_params=params,
        name="inner",
    )(source, coef)
    rim = pltpu.VMEM((2, 2 * WIDE + 1, comps, YE, width), F32)
    return pl.pallas_call(
        outer_kernel,
        out_shape=pltpu.HBM((harms, 2, size_x, size_y, width), F32),
        in_specs=[vmem] * 8,
        out_specs=hbm,
        scratch_shapes=[rim] * 4
        + [
            pltpu.VMEM((2, harms, 2, WIDE, size_y, width), F32),
            pltpu.SemaphoreType.DMA((3,)),
        ],
        compiler_params=params,
        name="outer",
    )(xlo, xhi, source, field1, field2, field3, inner, coef)


def solution(mesh):
    in_specs = (
        P("tm", ("sx", "sy"), None),
        P(("sx", "sy"), None),
        P(("sx", "sy")),
        P("sx", "sy", None),
        P(),
        P(),
    )
    out_specs = P("tm", None, "sx", "sy", None)
    return jax.shard_map(body, mesh=mesh, in_specs=in_specs, out_specs=out_specs, check_vma=False)
```

```python
import math

import jax
import jax.numpy as jnp
from jax import lax
from jax.experimental import pallas as pl
from jax.experimental.pallas import tpu as pltpu
from jax.sharding import PartitionSpec as P

TIME = 64
HARM = 32
NMAT = 4
CAP = 64
OWNERS = 32
WIDE = 3
Y0 = 4
YE = 24

omega_step = 0.1

F32 = jnp.float32
BF16 = jnp.bfloat16


def dft_table():
    freq_index = jnp.arange(HARM, dtype=jnp.int32)
    time_index = jnp.arange(TIME, dtype=jnp.int32)
    phase_int = freq_index[:, None] * time_index[None, :] % TIME
    angles = phase_int.astype(jnp.float32) * jnp.float32(2.0 * math.pi / TIME)
    amplitude = jnp.float32(2.0 / math.sqrt(TIME))
    table_rows = jnp.stack([amplitude * jnp.cos(angles), -amplitude * jnp.sin(angles)], axis=1)
    return table_rows.reshape(2 * HARM, TIME).astype(jnp.bfloat16)


def iota(shape, dim):
    return lax.broadcasted_iota(jnp.int32, shape, dim)


def pack_kernel(
    wall_hbm, owner_hbm, column_hbm, out_hbm, wall_ref, owner_ref, column_ref, stage_ref, in_sem, out_sem
):
    times, count, width = wall_ref.shape
    pulls = [
        pltpu.make_async_copy(source, target, in_sem.at[k])
        for k, (source, target) in enumerate(
            ((owner_hbm, owner_ref), (column_hbm, column_ref), (wall_hbm, wall_ref))
        )
    ]
    for pull in pulls:
        pull.start()
    before = (iota((width, width), 0) < iota((width, width), 1)).astype(F32).astype(BF16)
    pulls[0].wait()
    owner = owner_ref[...]
    hit = owner == iota((OWNERS, count), 0)
    hit_b = hit.astype(F32).astype(BF16)
    blocks = [hit_b[:, k * width : (k + 1) * width] for k in range(count // width)]
    earlier = jnp.dot(jnp.concatenate(blocks, axis=0), before, preferred_element_type=F32)
    carry = jnp.zeros((OWNERS, 1), F32)
    ranks = []
    for k, block in enumerate(blocks):
        inside = block.astype(F32)
        prefix = earlier[k * OWNERS : (k + 1) * OWNERS] + carry
        ranks.append(jnp.sum(inside * prefix, axis=0, keepdims=True))
        carry = carry + jnp.sum(inside, axis=1, keepdims=True)
    rank = jnp.concatenate(ranks, axis=1).astype(jnp.int32)
    pulls[1].wait()
    half = (rank == iota((CAP, count), 0)).astype(F32).astype(BF16)
    at_rank = jnp.concatenate([half, half], axis=0)
    marks = jnp.where(hit, (column_ref[...] + 1).astype(F32), 0.0).astype(BF16)
    columns = lax.dot_general(
        marks, at_rank, (((1,), (1,)), ((), ())), preferred_element_type=F32
    )
    stage_ref[:, times * CAP :, :] = jnp.broadcast_to(
        columns[:, None, :], (OWNERS, stage_ref.shape[1] - times * CAP, width)
    ).astype(BF16)
    pulls[2].wait()
    group = OWNERS // out_sem.shape[0]
    pushes = []
    for g in range(OWNERS // group):
        place = jnp.concatenate(
            [half * hit_b[o : o + 1, :] for o in range(g * group, (g + 1) * group)], axis=0
        )
        rows = jnp.concatenate([wall_ref[t] for t in range(times)], axis=1)
        moved = jnp.dot(place, rows, preferred_element_type=F32).astype(BF16)
        for t in range(times):
            stage_ref[g * group : (g + 1) * group, t * CAP : (t + 1) * CAP, :] = moved[
                :, t * width : (t + 1) * width
            ].reshape(group, CAP, width)
        push = pltpu.make_async_copy(
            stage_ref.at[pl.ds(g * group, group)], out_hbm.at[pl.ds(g * group, group)], out_sem.at[g]
        )
        push.start()
        pushes.append(push)
    for push in pushes:
        push.wait()


def sum_kernel(rows_ref, out_ref, *, times, cells):
    width = rows_ref.shape[2]
    side = out_ref.shape[1] // times
    acc = jnp.zeros((cells, times * width), F32)
    low = iota((1, width), 1) < CAP
    for g in range(OWNERS // 4):
        marks, rows = [], []
        for pair in range(2):
            i = g * 4 + pair * 2
            even = rows_ref[i, times * CAP : times * CAP + 8, :].astype(F32)[0:1]
            odd = rows_ref[i + 1, times * CAP : times * CAP + 8, :].astype(F32)[0:1]
            column = jnp.where(low, even, odd).astype(jnp.int32) - 1
            marks.append((column == iota((cells, width), 0)).astype(F32).astype(BF16))
            for j in range(2):
                rows.append(
                    jnp.concatenate(
                        [rows_ref[i + j, t * CAP : (t + 1) * CAP, :] for t in range(times)], axis=1
                    )
                )
        acc = acc + jnp.dot(
            jnp.concatenate(marks, axis=1),
            jnp.concatenate(rows, axis=0),
            preferred_element_type=F32,
        )
    total = acc.astype(BF16)
    for t in range(times):
        out_ref[:, t * side : (t + 1) * side, :] = total[:, t * width : (t + 1) * width].reshape(
            cells // side, side, width
        )


def weight_kernel(table_ref, out_ref):
    rows, cols = table_ref.shape
    side = out_ref.shape[0] // rows
    wide = rows * side
    spread = (iota((cols, wide), 1) // side == iota((cols, wide), 0)).astype(F32).astype(BF16)
    lift = (iota((wide, rows), 0) // side == iota((wide, rows), 1)).astype(F32).astype(BF16)
    wider = jnp.dot(table_ref[...], spread, preferred_element_type=F32).astype(BF16)
    step = 256
    for r in range(wide // step):
        full = jnp.dot(lift[r * step : (r + 1) * step], wider, preferred_element_type=F32)
        same = (iota((step, wide), 0) - iota((step, wide), 1)) % side == 0
        out_ref[r * step : (r + 1) * step, :] = jnp.where(same, full, 0.0).astype(BF16)


def dft_kernel(weights_ref, rows_ref, out_ref):
    times, side, width = rows_ref.shape
    half = side // 2
    rows = rows_ref[...].astype(F32)
    rows = jnp.concatenate(
        [rows[:, :half].reshape(times * half, width), rows[:, half:].reshape(times * half, width)], axis=1
    ).astype(BF16)
    made = jnp.dot(weights_ref[...], rows, preferred_element_type=F32)
    made = jnp.concatenate(
        [made[:, :width].reshape(times, half, width), made[:, width:].reshape(times, half, width)], axis=1
    )
    out_ref[...] = made.astype(BF16)


def coef_kernel(
    omega_ref, conductivity_ref, capacity_ref, south_ref, ids_ref, north_ref, coef_ref, mark_ref, c_ref
):
    ext_x, side, width = ids_ref.shape
    edge = south_ref.shape[1]
    ye = side + 2 * edge
    harms = omega_ref.shape[0]

    def table(ids, values):
        value = jnp.zeros((ye, width), F32)
        for m in range(NMAT):
            value = jnp.where(ids == m + 1, values[m], value)
        return value

    mark_ref[:, :edge] = south_ref[...].astype(F32)
    mark_ref[:, edge : edge + side] = ids_ref[...].astype(F32)
    mark_ref[:, edge + side :] = north_ref[...].astype(F32)

    def conduct_step(k, _):
        for i in (4 * k, 4 * k + 1, 4 * k + 2, 4 * k + 3):
            c_ref[i] = table(mark_ref[i], conductivity_ref)
        return 0

    lax.fori_loop(0, ext_x // 4, conduct_step, 0)

    def face(a, b):
        b = jnp.where(b > 0, b, a)
        both = a + b
        return 2.0 * a * b / jnp.where(both > 0, both, 1.0)

    lane = iota((ye, width), 1)

    def row(i, prev_x):
        c = c_ref[i + 1]
        next_x = face(c, c_ref[i + 2])
        next_y = face(c, pltpu.roll(c, ye - 1, 0))
        next_z = face(c, jnp.where(lane == width - 1, 0.0, pltpu.roll(c, width - 1, 1)))
        prev_y = jnp.where(pltpu.roll(c, 1, 0) > 0, pltpu.roll(next_y, 1, 0), c)
        prev_z = jnp.where(lane == 0, c, pltpu.roll(next_z, 1, 1))
        real_den = next_x + jnp.where(c_ref[i] > 0, prev_x, c) + next_y + prev_y + next_z + prev_z
        coef_ref[i, 0] = next_x
        coef_ref[i, 1] = next_y
        coef_ref[i, 2] = jnp.where(lane == width - 1, 0.0, next_z)
        mark = mark_ref[i + 1]
        heat = table(mark, capacity_ref)
        inside = mark > 0
        for h in range(harms):
            imag_den = omega_ref[h] * heat
            modulus = real_den * real_den + imag_den * imag_den
            inverse = jnp.where(inside, 1.0 / jnp.where(inside, modulus, 1.0), 0.0)
            coef_ref[i, 3 + 2 * h] = real_den * inverse
            coef_ref[i, 4 + 2 * h] = imag_den * inverse
        return next_x

    def step(k, prev_x):
        return row(2 * k + 1, row(2 * k, prev_x))

    lax.fori_loop(0, (ext_x - 2) // 2, step, face(c_ref[0], c_ref[1]))


def widen_kernel(mid_ref, ylo_ref, yhi_ref, s_ref, first_ref, last_ref):
    size_x, comps, ye, width = s_ref.shape
    wide = ylo_ref.shape[0]
    side = mid_ref.shape[1] // comps
    edge = jnp.zeros((size_x, comps, Y0 - wide, width), F32)
    s_ref[:, :, : Y0 - wide, :] = edge
    s_ref[:, :, ye - Y0 + wide :, :] = edge
    for c in range(comps):
        s_ref[:, c, Y0 : Y0 + side, :] = mid_ref[:, c * side : (c + 1) * side, :].astype(F32)
    for k in range(wide):
        for ref, start in ((ylo_ref, Y0 - wide + k), (yhi_ref, Y0 + side + k)):
            s_ref[:, :, start, :] = ref[k].astype(F32).reshape(size_x, comps, width)
    first_ref[...] = s_ref[:wide].reshape(wide, comps * ye, width).astype(BF16)
    last_ref[...] = s_ref[size_x - wide :].reshape(wide, comps * ye, width).astype(BF16)


def quotient(coef_ref, i, h, real_num, imag_num):
    a = coef_ref[i, 3 + 2 * h]
    b = coef_ref[i, 4 + 2 * h]
    return real_num * a + imag_num * b, imag_num * a - real_num * b


def sweep_row(coef_ref, source, field, i):
    ye, width = coef_ref.shape[2:]

    def numerator(c):
        here = field(i, c)
        fy = coef_ref[i, 1]
        fz = coef_ref[i, 2]
        total = source(c) + coef_ref[i, 0] * field(i + 1, c) + coef_ref[i - 1, 0] * field(i - 1, c)
        total = total + fy * pltpu.roll(here, ye - 1, 0) + pltpu.roll(fy * here, 1, 0)
        return total + fz * pltpu.roll(here, width - 1, 1) + pltpu.roll(fz * here, 1, 1)

    made = []
    for h in range((coef_ref.shape[1] - 3) // 2):
        made.extend(quotient(coef_ref, i, h, numerator(2 * h), numerator(2 * h + 1)))
    return made


def inner_kernel(s_ref, coef_ref, f1_ref, f2_ref, f3_ref, out_ref, *, wide):
    size_x, comps, ye, width = s_ref.shape
    side = out_ref.shape[3]

    def pairs(begin, end, row):
        def step(k, _):
            row(begin + 2 * k)
            row(begin + 2 * k + 1)
            return 0

        lax.fori_loop(0, (end - begin) // 2, step, 0)

    def first(x):
        for h in range(comps // 2):
            f1_ref[x, 2 * h], f1_ref[x, 2 * h + 1] = quotient(
                coef_ref, x + wide, h, s_ref[x, 2 * h], s_ref[x, 2 * h + 1]
            )

    pairs(0, size_x, first)

    def made(src, x):
        return sweep_row(
            coef_ref, lambda c: s_ref[x, c], lambda i, c: src[i - wide, c], x + wide
        )

    def sweep(src, dst, margin):
        def row(x):
            for c, value in enumerate(made(src, x)):
                dst[x, c] = value

        pairs(margin, size_x - margin, row)

    sweep(f1_ref, f2_ref, 1)
    sweep(f2_ref, f3_ref, 2)

    def last(x):
        for c, value in enumerate(made(f3_ref, x)):
            out_ref[c // 2, c % 2, x - wide] = value[Y0 : Y0 + side]

    pairs(wide, size_x - wide, last)


def outer_kernel(
    xlo_ref, xhi_ref, s_ref, f1_ref, f2_ref, f3_ref, inner_ref, coef_ref, out_hbm, s_rim, g1_ref, g2_ref, g3_ref, rim_ref, sem
):
    size_x, comps, ye, width = s_ref.shape
    wide = xlo_ref.shape[0]
    side = rim_ref.shape[4]
    ext_x = size_x + 2 * wide
    inner = pltpu.make_async_copy(
        inner_ref, out_hbm.at[:, :, pl.ds(wide, size_x - 2 * wide)], sem.at[0]
    )
    inner.start()
    span = 2 * wide + 1

    base = (0, ext_x - span)
    s_rim[0, :wide] = xlo_ref[...].astype(F32).reshape(wide, comps, ye, width)
    s_rim[0, wide : 2 * wide] = s_ref[:wide]
    s_rim[1, wide + 1 :] = xhi_ref[...].astype(F32).reshape(wide, comps, ye, width)
    s_rim[1, 1 : wide + 1] = s_ref[size_x - wide :]
    g1_ref[0, wide : wide + 2] = f1_ref[:2]
    g1_ref[1, wide - 1 : wide + 1] = f1_ref[size_x - 2 :]
    g2_ref[0, wide + 1 : wide + 3] = f2_ref[1:3]
    g2_ref[1, wide - 2 : wide] = f2_ref[size_x - 3 : size_x - 1]
    g3_ref[0, wide + 2 : wide + 4] = f3_ref[2:4]
    g3_ref[1, wide - 3 : wide - 1] = f3_ref[size_x - 4 : size_x - 2]

    def first(k, _):
        for part, j in ((0, k), (1, wide + 1 + k)):
            for h in range(comps // 2):
                g1_ref[part, j, 2 * h], g1_ref[part, j, 2 * h + 1] = quotient(
                    coef_ref, base[part] + j, h, s_rim[part, j, 2 * h], s_rim[part, j, 2 * h + 1]
                )
        return 0

    lax.fori_loop(0, wide, first, 0)

    def made(src, part, j):
        return sweep_row(
            coef_ref,
            lambda c: s_rim[part, j, c],
            lambda i, c: src[part, i - base[part], c],
            base[part] + j,
        )

    def sweep(src, dst, margin):
        def step(k, _):
            for part, j in ((0, margin + k), (1, wide + 1 - margin + k)):
                for c, value in enumerate(made(src, part, j)):
                    dst[part, j, c] = value
            return 0

        lax.fori_loop(0, wide, step, 0)

    sweep(g1_ref, g2_ref, 1)
    sweep(g2_ref, g3_ref, 2)

    def last(k, _):
        for part, j in ((0, wide + k), (1, 1 + k)):
            for c, value in enumerate(made(g3_ref, part, j)):
                rim_ref[part, c // 2, c % 2, k] = value[Y0 : Y0 + side]
        return 0

    lax.fori_loop(0, wide, last, 0)
    low = pltpu.make_async_copy(rim_ref.at[0], out_hbm.at[:, :, pl.ds(0, wide)], sem.at[1])
    high = pltpu.make_async_copy(rim_ref.at[1], out_hbm.at[:, :, pl.ds(size_x - wide, wide)], sem.at[2])
    low.start()
    high.start()
    inner.wait()
    low.wait()
    high.wait()


def swap(block, axis, dim, width):
    count = lax.axis_size(axis)
    forward = [(i, i + 1) for i in range(count - 1)]
    backward = [(target, source) for source, target in forward]
    size = block.shape[dim]
    low = lax.ppermute(lax.slice_in_dim(block, size - width, size, axis=dim), axis, forward)
    high = lax.ppermute(lax.slice_in_dim(block, 0, width, axis=dim), axis, backward)
    return low, high


def body(wall_temp, owner_map, stencil_column, material, conductivity, capacity):
    times, count, width = wall_temp.shape
    size_x, size_y, _ = material.shape
    steps = lax.axis_size("tm")
    comps = 2 * HARM // steps
    harms = comps // 2
    ext_x = size_x + 2 * WIDE
    params = pltpu.CompilerParams(vmem_limit_bytes=16 * 1024 * 1024)
    vmem = pl.BlockSpec(memory_space=pltpu.VMEM)
    smem = pl.BlockSpec(memory_space=pltpu.SMEM)

    hbm = pl.BlockSpec(memory_space=pltpu.HBM)
    packed = pl.pallas_call(
        pack_kernel,
        out_shape=pltpu.HBM((OWNERS, times * CAP + 8, width), BF16),
        in_specs=[hbm] * 3,
        out_specs=hbm,
        scratch_shapes=[
            pltpu.VMEM((times, count, width), BF16),
            pltpu.VMEM((1, count), jnp.int32),
            pltpu.VMEM((1, count), jnp.int32),
            pltpu.VMEM((OWNERS, times * CAP + 8, width), BF16),
            pltpu.SemaphoreType.DMA((3,)),
            pltpu.SemaphoreType.DMA((8,)),
        ],
        compiler_params=params,
        name="pack",
    )(
        *(
            pltpu.with_memory_space_constraint(operand, pltpu.HBM)
            for operand in (wall_temp, owner_map.reshape(1, count), stencil_column.reshape(1, count))
        )
    )
    received = lax.all_to_all(packed, ("sx", "sy"), split_axis=0, concat_axis=0, tiled=True)

    table, material = lax.optimization_barrier((dft_table(), material))
    weights = pl.pallas_call(
        weight_kernel,
        out_shape=jax.ShapeDtypeStruct((TIME * size_y // 2, TIME * size_y // 2), BF16),
        in_specs=[vmem],
        out_specs=vmem,
        compiler_params=params,
        name="weights",
    )(table)
    material, weights = lax.optimization_barrier((material, weights))
    ids = (material + 1).astype(BF16)
    west, east = swap(ids, "sx", 0, Y0)
    received, west, east = lax.optimization_barrier((received, west, east))
    ids = jnp.concatenate([west, ids, east], axis=0)
    south, north = swap(ids, "sy", 1, Y0)
    cells = size_x * size_y
    sums = pl.pallas_call(
        lambda *refs: sum_kernel(*refs, times=times, cells=cells),
        out_shape=jax.ShapeDtypeStruct((size_x, times * size_y, width), BF16),
        in_specs=[vmem],
        out_specs=vmem,
        compiler_params=params,
        name="cell_sum",
    )(received)
    gathered = lax.all_to_all(sums, "tm", split_axis=0, concat_axis=0, tiled=True)
    gathered, ids, south, north = lax.optimization_barrier((gathered, ids, south, north))
    harmonic = pl.pallas_call(
        dft_kernel,
        out_shape=jax.ShapeDtypeStruct((TIME, size_y, width), BF16),
        in_specs=[vmem] * 2,
        out_specs=vmem,
        compiler_params=params,
        name="dft",
    )(weights, gathered.reshape(TIME, size_y, width))
    harmonic = harmonic.reshape(steps, comps * size_y, width)
    source = lax.all_to_all(harmonic, "tm", split_axis=0, concat_axis=0, tiled=True)
    source, south, ids, north = lax.optimization_barrier((source, south, ids, north))

    rows = source.reshape(size_x, comps, size_y, width)
    rows = jnp.concatenate([rows[:, :, :WIDE], rows[:, :, size_y - WIDE :]], axis=2)
    rows = jnp.transpose(rows, (2, 0, 1, 3)).reshape(2 * WIDE, size_x * comps, width)
    ylo, yhi = swap(rows, "sy", 0, WIDE)
    harm_index = lax.axis_index("tm") * harms + jnp.arange(harms, dtype=jnp.int32)
    omega = omega_step * harm_index.astype(F32)
    coef = pl.pallas_call(
        coef_kernel,
        out_shape=jax.ShapeDtypeStruct((ext_x, 3 + 2 * harms, YE, width), F32),
        in_specs=[smem] * 3 + [vmem] * 3,
        out_specs=vmem,
        scratch_shapes=[pltpu.VMEM((ext_x + 2, YE, width), F32)] * 2,
        compiler_params=params,
        name="coef",
    )(omega, conductivity, capacity, south, ids, north)
    ylo, yhi, coef = lax.optimization_barrier((ylo, yhi, coef))
    widened = jax.ShapeDtypeStruct((size_x, comps, YE, width), F32)
    strip = jax.ShapeDtypeStruct((WIDE, comps * YE, width), BF16)
    source, first_rows, last_rows = pl.pallas_call(
        widen_kernel,
        out_shape=[widened, strip, strip],
        in_specs=[vmem] * 3,
        out_specs=[vmem] * 3,
        compiler_params=params,
        name="widen",
    )(source, ylo, yhi)
    count_x = lax.axis_size("sx")
    forward = [(i, i + 1) for i in range(count_x - 1)]
    backward = [(target, start) for start, target in forward]
    xlo = lax.ppermute(last_rows, "sx", forward)
    xhi = lax.ppermute(first_rows, "sx", backward)
    field1, field2, field3, inner = pl.pallas_call(
        lambda *refs: inner_kernel(*refs, wide=WIDE),
        out_shape=[widened] * 3
        + [jax.ShapeDtypeStruct((harms, 2, size_x - 2 * WIDE, size_y, width), F32)],
        in_specs=[vmem] * 2,
        out_specs=[vmem] * 4,
        compiler_params=params,
        name="inner",
    )(source, coef)
    rim = pltpu.VMEM((2, 2 * WIDE + 1, comps, YE, width), F32)
    return pl.pallas_call(
        outer_kernel,
        out_shape=pltpu.HBM((harms, 2, size_x, size_y, width), F32),
        in_specs=[vmem] * 8,
        out_specs=hbm,
        scratch_shapes=[rim] * 4
        + [
            pltpu.VMEM((2, harms, 2, WIDE, size_y, width), F32),
            pltpu.SemaphoreType.DMA((3,)),
        ],
        compiler_params=params,
        name="outer",
    )(xlo, xhi, source, field1, field2, field3, inner, coef)


def solution(mesh):
    in_specs = (
        P("tm", ("sx", "sy"), None),
        P(("sx", "sy"), None),
        P(("sx", "sy")),
        P("sx", "sy", None),
        P(),
        P(),
    )
    out_specs = P("tm", None, "sx", "sy", None)
    return jax.shard_map(body, mesh=mesh, in_specs=in_specs, out_specs=out_specs, check_vma=False)
```

```python
import math

import jax
import jax.numpy as jnp
from jax import lax
from jax.experimental import pallas as pl
from jax.experimental.pallas import tpu as pltpu
from jax.sharding import PartitionSpec as P

TIME = 64
HARM = 32
NMAT = 4
CAP = 64
OWNERS = 32
WIDE = 3
Y0 = 4
YE = 24

omega_step = 0.1

F32 = jnp.float32
BF16 = jnp.bfloat16


def dft_table():
    freq_index = jnp.arange(HARM, dtype=jnp.int32)
    time_index = jnp.arange(TIME, dtype=jnp.int32)
    phase_int = freq_index[:, None] * time_index[None, :] % TIME
    angles = phase_int.astype(jnp.float32) * jnp.float32(2.0 * math.pi / TIME)
    amplitude = jnp.float32(2.0 / math.sqrt(TIME))
    table_rows = jnp.stack([amplitude * jnp.cos(angles), -amplitude * jnp.sin(angles)], axis=1)
    return table_rows.reshape(2 * HARM, TIME).astype(jnp.bfloat16)


def iota(shape, dim):
    return lax.broadcasted_iota(jnp.int32, shape, dim)


def pack_kernel(
    wall_hbm, owner_hbm, column_hbm, out_hbm, wall_ref, owner_ref, column_ref, stage_ref, in_sem, out_sem
):
    times, count, width = wall_ref.shape
    pulls = [
        pltpu.make_async_copy(source, target, in_sem.at[k])
        for k, (source, target) in enumerate(
            ((owner_hbm, owner_ref), (column_hbm, column_ref), (wall_hbm, wall_ref))
        )
    ]
    for pull in pulls:
        pull.start()
    before = (iota((width, width), 0) < iota((width, width), 1)).astype(F32).astype(BF16)
    pulls[0].wait()
    owner = owner_ref[...]
    hit = owner == iota((OWNERS, count), 0)
    hit_b = hit.astype(F32).astype(BF16)
    blocks = [hit_b[:, k * width : (k + 1) * width] for k in range(count // width)]
    earlier = jnp.dot(jnp.concatenate(blocks, axis=0), before, preferred_element_type=F32)
    carry = jnp.zeros((OWNERS, 1), F32)
    ranks = []
    for k, block in enumerate(blocks):
        inside = block.astype(F32)
        prefix = earlier[k * OWNERS : (k + 1) * OWNERS] + carry
        ranks.append(jnp.sum(inside * prefix, axis=0, keepdims=True))
        carry = carry + jnp.sum(inside, axis=1, keepdims=True)
    rank = jnp.concatenate(ranks, axis=1).astype(jnp.int32)
    pulls[1].wait()
    half = (rank == iota((CAP, count), 0)).astype(F32).astype(BF16)
    at_rank = jnp.concatenate([half, half], axis=0)
    marks = jnp.where(hit, (column_ref[...] + 1).astype(F32), 0.0).astype(BF16)
    columns = lax.dot_general(
        marks, at_rank, (((1,), (1,)), ((), ())), preferred_element_type=F32
    )
    stage_ref[:, times * CAP :, :] = jnp.broadcast_to(
        columns[:, None, :], (OWNERS, stage_ref.shape[1] - times * CAP, width)
    ).astype(BF16)
    pulls[2].wait()
    group = OWNERS // out_sem.shape[0]
    pushes = []
    for g in range(OWNERS // group):
        place = jnp.concatenate(
            [half * hit_b[o : o + 1, :] for o in range(g * group, (g + 1) * group)], axis=0
        )
        rows = jnp.concatenate([wall_ref[t] for t in range(times)], axis=1)
        moved = jnp.dot(place, rows, preferred_element_type=F32).astype(BF16)
        for t in range(times):
            stage_ref[g * group : (g + 1) * group, t * CAP : (t + 1) * CAP, :] = moved[
                :, t * width : (t + 1) * width
            ].reshape(group, CAP, width)
        push = pltpu.make_async_copy(
            stage_ref.at[pl.ds(g * group, group)], out_hbm.at[pl.ds(g * group, group)], out_sem.at[g]
        )
        push.start()
        pushes.append(push)
    for push in pushes:
        push.wait()


def sum_kernel(rows_ref, out_ref, *, times, cells):
    width = rows_ref.shape[2]
    side = out_ref.shape[1] // times
    acc = jnp.zeros((cells, times * width), F32)
    low = iota((1, width), 1) < CAP
    for g in range(OWNERS // 4):
        marks, rows = [], []
        for pair in range(2):
            i = g * 4 + pair * 2
            even = rows_ref[i, times * CAP : times * CAP + 8, :].astype(F32)[0:1]
            odd = rows_ref[i + 1, times * CAP : times * CAP + 8, :].astype(F32)[0:1]
            column = jnp.where(low, even, odd).astype(jnp.int32) - 1
            marks.append((column == iota((cells, width), 0)).astype(F32).astype(BF16))
            for j in range(2):
                rows.append(
                    jnp.concatenate(
                        [rows_ref[i + j, t * CAP : (t + 1) * CAP, :] for t in range(times)], axis=1
                    )
                )
        acc = acc + jnp.dot(
            jnp.concatenate(marks, axis=1),
            jnp.concatenate(rows, axis=0),
            preferred_element_type=F32,
        )
    total = acc.astype(BF16)
    for t in range(times):
        out_ref[:, t * side : (t + 1) * side, :] = total[:, t * width : (t + 1) * width].reshape(
            cells // side, side, width
        )


def weight_kernel(table_ref, out_ref):
    rows, cols = table_ref.shape
    side = out_ref.shape[0] // rows
    wide = rows * side
    spread = (iota((cols, wide), 1) // side == iota((cols, wide), 0)).astype(F32).astype(BF16)
    lift = (iota((wide, rows), 0) // side == iota((wide, rows), 1)).astype(F32).astype(BF16)
    wider = jnp.dot(table_ref[...], spread, preferred_element_type=F32).astype(BF16)
    step = 256
    for r in range(wide // step):
        full = jnp.dot(lift[r * step : (r + 1) * step], wider, preferred_element_type=F32)
        same = (iota((step, wide), 0) - iota((step, wide), 1)) % side == 0
        out_ref[r * step : (r + 1) * step, :] = jnp.where(same, full, 0.0).astype(BF16)


def dft_kernel(weights_ref, rows_ref, out_ref):
    times, side, width = rows_ref.shape
    half = side // 2
    rows = rows_ref[...].astype(F32)
    rows = jnp.concatenate(
        [rows[:, :half].reshape(times * half, width), rows[:, half:].reshape(times * half, width)], axis=1
    ).astype(BF16)
    made = jnp.dot(weights_ref[...], rows, preferred_element_type=F32)
    made = jnp.concatenate(
        [made[:, :width].reshape(times, half, width), made[:, width:].reshape(times, half, width)], axis=1
    )
    out_ref[...] = made.astype(BF16)


def coef_kernel(
    omega_ref, conductivity_ref, capacity_ref, south_ref, ids_ref, north_ref, coef_ref, mark_ref, c_ref
):
    ext_x, side, width = ids_ref.shape
    edge = south_ref.shape[1]
    ye = side + 2 * edge
    harms = omega_ref.shape[0]

    def table(ids, values):
        value = jnp.zeros((ye, width), F32)
        for m in range(NMAT):
            value = jnp.where(ids == m + 1, values[m], value)
        return value

    mark_ref[:, :edge] = south_ref[...].astype(F32)
    mark_ref[:, edge : edge + side] = ids_ref[...].astype(F32)
    mark_ref[:, edge + side :] = north_ref[...].astype(F32)

    def conduct_step(k, _):
        for i in (4 * k, 4 * k + 1, 4 * k + 2, 4 * k + 3):
            c_ref[i] = table(mark_ref[i], conductivity_ref)
        return 0

    lax.fori_loop(0, ext_x // 4, conduct_step, 0)

    def face(a, b):
        b = jnp.where(b > 0, b, a)
        both = a + b
        return 2.0 * a * b / jnp.where(both > 0, both, 1.0)

    lane = iota((ye, width), 1)

    def row(i, prev_x):
        c = c_ref[i + 1]
        next_x = face(c, c_ref[i + 2])
        next_y = face(c, pltpu.roll(c, ye - 1, 0))
        next_z = face(c, jnp.where(lane == width - 1, 0.0, pltpu.roll(c, width - 1, 1)))
        prev_y = jnp.where(pltpu.roll(c, 1, 0) > 0, pltpu.roll(next_y, 1, 0), c)
        prev_z = jnp.where(lane == 0, c, pltpu.roll(next_z, 1, 1))
        real_den = next_x + jnp.where(c_ref[i] > 0, prev_x, c) + next_y + prev_y + next_z + prev_z
        coef_ref[i, 0] = next_x
        coef_ref[i, 1] = next_y
        coef_ref[i, 2] = jnp.where(lane == width - 1, 0.0, next_z)
        mark = mark_ref[i + 1]
        heat = table(mark, capacity_ref)
        inside = mark > 0
        for h in range(harms):
            imag_den = omega_ref[h] * heat
            modulus = real_den * real_den + imag_den * imag_den
            inverse = jnp.where(inside, 1.0 / jnp.where(inside, modulus, 1.0), 0.0)
            coef_ref[i, 3 + 2 * h] = real_den * inverse
            coef_ref[i, 4 + 2 * h] = imag_den * inverse
        return next_x

    def step(k, prev_x):
        return row(2 * k + 1, row(2 * k, prev_x))

    lax.fori_loop(0, (ext_x - 2) // 2, step, face(c_ref[0], c_ref[1]))


def widen_kernel(mid_ref, ylo_ref, yhi_ref, s_ref, first_ref, last_ref):
    size_x, comps, ye, width = s_ref.shape
    wide = ylo_ref.shape[0]
    side = mid_ref.shape[1] // comps
    edge = jnp.zeros((size_x, comps, Y0 - wide, width), F32)
    s_ref[:, :, : Y0 - wide, :] = edge
    s_ref[:, :, ye - Y0 + wide :, :] = edge
    for c in range(comps):
        s_ref[:, c, Y0 : Y0 + side, :] = mid_ref[:, c * side : (c + 1) * side, :].astype(F32)
    for k in range(wide):
        for ref, start in ((ylo_ref, Y0 - wide + k), (yhi_ref, Y0 + side + k)):
            s_ref[:, :, start, :] = ref[k].astype(F32).reshape(size_x, comps, width)
    first_ref[...] = s_ref[:wide].reshape(wide, comps * ye, width).astype(BF16)
    last_ref[...] = s_ref[size_x - wide :].reshape(wide, comps * ye, width).astype(BF16)


def quotient(coef_ref, i, h, real_num, imag_num):
    a = coef_ref[i, 3 + 2 * h]
    b = coef_ref[i, 4 + 2 * h]
    return real_num * a + imag_num * b, imag_num * a - real_num * b


def sweep_row(coef_ref, source, field, i):
    ye, width = coef_ref.shape[2:]

    def numerator(c):
        here = field(i, c)
        fy = coef_ref[i, 1]
        fz = coef_ref[i, 2]
        total = source(c) + coef_ref[i, 0] * field(i + 1, c) + coef_ref[i - 1, 0] * field(i - 1, c)
        total = total + fy * pltpu.roll(here, ye - 1, 0) + pltpu.roll(fy * here, 1, 0)
        return total + fz * pltpu.roll(here, width - 1, 1) + pltpu.roll(fz * here, 1, 1)

    made = []
    for h in range((coef_ref.shape[1] - 3) // 2):
        made.extend(quotient(coef_ref, i, h, numerator(2 * h), numerator(2 * h + 1)))
    return made


def inner_kernel(s_ref, coef_ref, f1_ref, f2_ref, f3_ref, out_ref, *, wide):
    size_x, comps, ye, width = s_ref.shape
    side = out_ref.shape[3]

    def pairs(begin, end, row):
        def step(k, _):
            row(begin + 2 * k)
            row(begin + 2 * k + 1)
            return 0

        lax.fori_loop(0, (end - begin) // 2, step, 0)

    def first(x):
        for h in range(comps // 2):
            f1_ref[x, 2 * h], f1_ref[x, 2 * h + 1] = quotient(
                coef_ref, x + wide, h, s_ref[x, 2 * h], s_ref[x, 2 * h + 1]
            )

    pairs(0, size_x, first)

    def made(src, x):
        return sweep_row(
            coef_ref, lambda c: s_ref[x, c], lambda i, c: src[i - wide, c], x + wide
        )

    def sweep(src, dst, margin):
        def row(x):
            for c, value in enumerate(made(src, x)):
                dst[x, c] = value

        pairs(margin, size_x - margin, row)

    sweep(f1_ref, f2_ref, 1)
    sweep(f2_ref, f3_ref, 2)

    def last(x):
        for c, value in enumerate(made(f3_ref, x)):
            out_ref[c // 2, c % 2, x - wide] = value[Y0 : Y0 + side]

    pairs(wide, size_x - wide, last)


def outer_kernel(
    xlo_ref, xhi_ref, s_ref, f1_ref, f2_ref, f3_ref, inner_ref, coef_ref, out_hbm, s_rim, g1_ref, g2_ref, g3_ref, rim_ref, sem
):
    size_x, comps, ye, width = s_ref.shape
    wide = xlo_ref.shape[0]
    side = rim_ref.shape[4]
    ext_x = size_x + 2 * wide
    inner = pltpu.make_async_copy(
        inner_ref, out_hbm.at[:, :, pl.ds(wide, size_x - 2 * wide)], sem.at[0]
    )
    inner.start()
    span = 2 * wide + 1

    base = (0, ext_x - span)
    s_rim[0, :wide] = xlo_ref[...].astype(F32).reshape(wide, comps, ye, width)
    s_rim[0, wide : 2 * wide] = s_ref[:wide]
    s_rim[1, wide + 1 :] = xhi_ref[...].astype(F32).reshape(wide, comps, ye, width)
    s_rim[1, 1 : wide + 1] = s_ref[size_x - wide :]
    g1_ref[0, wide : wide + 2] = f1_ref[:2]
    g1_ref[1, wide - 1 : wide + 1] = f1_ref[size_x - 2 :]
    g2_ref[0, wide + 1 : wide + 3] = f2_ref[1:3]
    g2_ref[1, wide - 2 : wide] = f2_ref[size_x - 3 : size_x - 1]
    g3_ref[0, wide + 2 : wide + 4] = f3_ref[2:4]
    g3_ref[1, wide - 3 : wide - 1] = f3_ref[size_x - 4 : size_x - 2]

    def first(k, _):
        for part, j in ((0, k), (1, wide + 1 + k)):
            for h in range(comps // 2):
                g1_ref[part, j, 2 * h], g1_ref[part, j, 2 * h + 1] = quotient(
                    coef_ref, base[part] + j, h, s_rim[part, j, 2 * h], s_rim[part, j, 2 * h + 1]
                )
        return 0

    lax.fori_loop(0, wide, first, 0)

    def made(src, part, j):
        return sweep_row(
            coef_ref,
            lambda c: s_rim[part, j, c],
            lambda i, c: src[part, i - base[part], c],
            base[part] + j,
        )

    def sweep(src, dst, margin):
        def step(k, _):
            for part, j in ((0, margin + k), (1, wide + 1 - margin + k)):
                for c, value in enumerate(made(src, part, j)):
                    dst[part, j, c] = value
            return 0

        lax.fori_loop(0, wide, step, 0)

    sweep(g1_ref, g2_ref, 1)
    sweep(g2_ref, g3_ref, 2)

    def last(k, _):
        for part, j in ((0, wide + k), (1, 1 + k)):
            for c, value in enumerate(made(g3_ref, part, j)):
                rim_ref[part, c // 2, c % 2, k] = value[Y0 : Y0 + side]
        return 0

    lax.fori_loop(0, wide, last, 0)
    low = pltpu.make_async_copy(rim_ref.at[0], out_hbm.at[:, :, pl.ds(0, wide)], sem.at[1])
    high = pltpu.make_async_copy(rim_ref.at[1], out_hbm.at[:, :, pl.ds(size_x - wide, wide)], sem.at[2])
    low.start()
    high.start()
    inner.wait()
    low.wait()
    high.wait()


def swap(block, axis, dim, width):
    count = lax.axis_size(axis)
    forward = [(i, i + 1) for i in range(count - 1)]
    backward = [(target, source) for source, target in forward]
    size = block.shape[dim]
    low = lax.ppermute(lax.slice_in_dim(block, size - width, size, axis=dim), axis, forward)
    high = lax.ppermute(lax.slice_in_dim(block, 0, width, axis=dim), axis, backward)
    return low, high


def body(wall_temp, owner_map, stencil_column, material, conductivity, capacity):
    times, count, width = wall_temp.shape
    size_x, size_y, _ = material.shape
    steps = lax.axis_size("tm")
    comps = 2 * HARM // steps
    harms = comps // 2
    ext_x = size_x + 2 * WIDE
    params = pltpu.CompilerParams(vmem_limit_bytes=16 * 1024 * 1024)
    vmem = pl.BlockSpec(memory_space=pltpu.VMEM)
    smem = pl.BlockSpec(memory_space=pltpu.SMEM)

    hbm = pl.BlockSpec(memory_space=pltpu.HBM)
    packed = pl.pallas_call(
        pack_kernel,
        out_shape=pltpu.HBM((OWNERS, times * CAP + 8, width), BF16),
        in_specs=[hbm] * 3,
        out_specs=hbm,
        scratch_shapes=[
            pltpu.VMEM((times, count, width), BF16),
            pltpu.VMEM((1, count), jnp.int32),
            pltpu.VMEM((1, count), jnp.int32),
            pltpu.VMEM((OWNERS, times * CAP + 8, width), BF16),
            pltpu.SemaphoreType.DMA((3,)),
            pltpu.SemaphoreType.DMA((8,)),
        ],
        compiler_params=params,
        name="pack",
    )(
        *(
            pltpu.with_memory_space_constraint(operand, pltpu.HBM)
            for operand in (wall_temp, owner_map.reshape(1, count), stencil_column.reshape(1, count))
        )
    )
    received = lax.all_to_all(packed, ("sx", "sy"), split_axis=0, concat_axis=0, tiled=True)

    table, material = lax.optimization_barrier((dft_table(), material))
    weights = pl.pallas_call(
        weight_kernel,
        out_shape=jax.ShapeDtypeStruct((TIME * size_y // 2, TIME * size_y // 2), BF16),
        in_specs=[vmem],
        out_specs=vmem,
        compiler_params=params,
        name="weights",
    )(table)
    material, weights = lax.optimization_barrier((material, weights))
    ids = (material + 1).astype(BF16)
    west, east = swap(ids, "sx", 0, Y0)
    received, west, east = lax.optimization_barrier((received, west, east))
    ids = jnp.concatenate([west, ids, east], axis=0)
    south, north = swap(ids, "sy", 1, Y0)
    cells = size_x * size_y
    sums = pl.pallas_call(
        lambda *refs: sum_kernel(*refs, times=times, cells=cells),
        out_shape=jax.ShapeDtypeStruct((size_x, times * size_y, width), BF16),
        in_specs=[vmem],
        out_specs=vmem,
        compiler_params=params,
        name="cell_sum",
    )(received)
    gathered = lax.all_to_all(sums, "tm", split_axis=0, concat_axis=0, tiled=True)
    gathered, ids, south, north = lax.optimization_barrier((gathered, ids, south, north))
    harmonic = pl.pallas_call(
        dft_kernel,
        out_shape=jax.ShapeDtypeStruct((TIME, size_y, width), BF16),
        in_specs=[vmem] * 2,
        out_specs=vmem,
        compiler_params=params,
        name="dft",
    )(weights, gathered.reshape(TIME, size_y, width))
    harmonic = harmonic.reshape(steps, comps * size_y, width)
    source = lax.all_to_all(harmonic, "tm", split_axis=0, concat_axis=0, tiled=True)
    harm_index = lax.axis_index("tm") * harms + jnp.arange(harms, dtype=jnp.int32)
    omega = omega_step * harm_index.astype(F32)
    coef = pl.pallas_call(
        coef_kernel,
        out_shape=jax.ShapeDtypeStruct((ext_x, 3 + 2 * harms, YE, width), F32),
        in_specs=[smem] * 3 + [vmem] * 3,
        out_specs=vmem,
        scratch_shapes=[pltpu.VMEM((ext_x + 2, YE, width), F32)] * 2,
        compiler_params=params,
        name="coef",
    )(omega, conductivity, capacity, south, ids, north)
    source, coef = lax.optimization_barrier((source, coef))

    rows = source.reshape(size_x, comps, size_y, width)
    rows = jnp.concatenate([rows[:, :, :WIDE], rows[:, :, size_y - WIDE :]], axis=2)
    rows = jnp.transpose(rows, (2, 0, 1, 3)).reshape(2 * WIDE, size_x * comps, width)
    ylo, yhi = swap(rows, "sy", 0, WIDE)
    widened = jax.ShapeDtypeStruct((size_x, comps, YE, width), F32)
    strip = jax.ShapeDtypeStruct((WIDE, comps * YE, width), BF16)
    source, first_rows, last_rows = pl.pallas_call(
        widen_kernel,
        out_shape=[widened, strip, strip],
        in_specs=[vmem] * 3,
        out_specs=[vmem] * 3,
        compiler_params=params,
        name="widen",
    )(source, ylo, yhi)
    count_x = lax.axis_size("sx")
    forward = [(i, i + 1) for i in range(count_x - 1)]
    backward = [(target, start) for start, target in forward]
    xlo = lax.ppermute(last_rows, "sx", forward)
    xhi = lax.ppermute(first_rows, "sx", backward)
    field1, field2, field3, inner = pl.pallas_call(
        lambda *refs: inner_kernel(*refs, wide=WIDE),
        out_shape=[widened] * 3
        + [jax.ShapeDtypeStruct((harms, 2, size_x - 2 * WIDE, size_y, width), F32)],
        in_specs=[vmem] * 2,
        out_specs=[vmem] * 4,
        compiler_params=params,
        name="inner",
    )(source, coef)
    rim = pltpu.VMEM((2, 2 * WIDE + 1, comps, YE, width), F32)
    return pl.pallas_call(
        outer_kernel,
        out_shape=pltpu.HBM((harms, 2, size_x, size_y, width), F32),
        in_specs=[vmem] * 8,
        out_specs=hbm,
        scratch_shapes=[rim] * 4
        + [
            pltpu.VMEM((2, harms, 2, WIDE, size_y, width), F32),
            pltpu.SemaphoreType.DMA((3,)),
        ],
        compiler_params=params,
        name="outer",
    )(xlo, xhi, source, field1, field2, field3, inner, coef)


def solution(mesh):
    in_specs = (
        P("tm", ("sx", "sy"), None),
        P(("sx", "sy"), None),
        P(("sx", "sy")),
        P("sx", "sy", None),
        P(),
        P(),
    )
    out_specs = P("tm", None, "sx", "sy", None)
    return jax.shard_map(body, mesh=mesh, in_specs=in_specs, out_specs=out_specs, check_vma=False)
```
